32 devices in a mesh: dp: 8 (over z, core), tensor: 4 (over y, x).
Axes of the slice: x: 2, y: 2, z: 4, core: 2. Of those that a mesh axis runs over, the one named last changes fastest.
Arguments:
- tokens: bfloat16 [16384, 2048], P(('dp', 'tensor')), may hold values from -6 to 6
- cotangent: bfloat16 [16384, 2048], P(('dp', 'tensor')), may hold values from -6 to 6
- seq_ids: int32 [16384], P('dp'), may hold values from 0 to 15, as said below
- block_ids: int32 [16384], P('dp'), may hold values from 0 to 7, as said below
- groups: int32 [8], replicated, may hold values from 0 to 3, as said below
- qkv_weight: float32 [3, 2048, 2048], P(None, 'dp', 'tensor'), may hold values from -0.125 to 0.125
- out_weight: float32 [2048, 2048], P('tensor', 'dp'), may hold values from -2 to 2
- gate_weight: float32 [2, 2048, 8192], P(None, 'dp', 'tensor'), may hold values from -0.125 to 0.125
- down_weight: float32 [8192, 2048], P('tensor', 'dp'), may hold values from -0.0625 to 0.0625
- norm_gains: float32 [2, 2048], replicated, may hold values from 0.5 to 1.5
- qkv_first: float32 [4, 3, 2048, 2048], P(None, None, 'dp', 'tensor'), may hold values from -24 to 24
- out_first: float32 [4, 2048, 2048], P(None, 'tensor', 'dp'), may hold values from -6 to 6
- gate_first: float32 [4, 2, 2048, 8192], P(None, None, 'dp', 'tensor'), may hold values from -6 to 6
- down_first: float32 [4, 8192, 2048], P(None, 'tensor', 'dp'), may hold values from -24 to 24
- gains_first: float32 [4, 2, 2048], replicated, may hold values from -32 to 32
- qkv_second: float32 [4, 3, 2048, 2048], P(None, None, 'dp', 'tensor'), may hold values from 77.824 to 311.296
- out_second: float32 [4, 2048, 2048], P(None, 'tensor', 'dp'), may hold values from 0.77824 to 3.11296
- gate_second: float32 [4, 2, 2048, 8192], P(None, None, 'dp', 'tensor'), may hold values from 13.5168 to 53.248
- down_second: float32 [4, 8192, 2048], P(None, 'tensor', 'dp'), may hold values from 77.824 to 311.296
- gains_second: float32 [4, 2, 2048], replicated, may hold values from 106.496 to 409.6
- qkv_outer: float32 [3, 2048, 2048], P(None, 'dp', 'tensor'), may hold values from -0.1875 to 0.1875
- out_outer: float32 [2048, 2048], P('tensor', 'dp'), may hold values from -2.5 to 2.5
- gate_outer: float32 [2, 2048, 8192], P(None, 'dp', 'tensor'), may hold values from -0.1875 to 0.1875
- down_outer: float32 [8192, 2048], P('tensor', 'dp'), may hold values from -0.09375 to 0.09375
- gains_outer: float32 [2, 2048], replicated, may hold values from -1.5 to 1.5
Outputs:
- layer_out: bfloat16 [16384, 2048], P(('dp', 'tensor'))
- tokens_grad: float32 [16384, 2048], P(('dp', 'tensor'))
- qkv_first_new: float32 [4, 3, 2048, 2048], P(None, None, 'dp', 'tensor')
- qkv_second_new: float32 [4, 3, 2048, 2048], P(None, None, 'dp', 'tensor')
- qkv_delta: float32 [3, 2048, 2048], P(None, 'dp', 'tensor')
- qkv_outer_new: float32 [3, 2048, 2048], P(None, 'dp', 'tensor')
- qkv_master: float32 [3, 2048, 2048], P(None, 'dp', 'tensor')
- qkv_low: bfloat16 [3, 2048, 2048], P(None, 'dp', 'tensor')
- out_first_new: float32 [4, 2048, 2048], P(None, 'tensor', 'dp')
- out_second_new: float32 [4, 2048, 2048], P(None, 'tensor', 'dp')
- out_delta: float32 [2048, 2048], P('tensor', 'dp')
- out_outer_new: float32 [2048, 2048], P('tensor', 'dp')
- out_master: float32 [2048, 2048], P('tensor', 'dp')
- out_low: bfloat16 [2048, 2048], P('tensor', 'dp')
- gate_first_new: float32 [4, 2, 2048, 8192], P(None, None, 'dp', 'tensor')
- gate_second_new: float32 [4, 2, 2048, 8192], P(None, None, 'dp', 'tensor')
- gate_delta: float32 [2, 2048, 8192], P(None, 'dp', 'tensor')
- gate_outer_new: float32 [2, 2048, 8192], P(None, 'dp', 'tensor')
- gate_master: float32 [2, 2048, 8192], P(None, 'dp', 'tensor')
- gate_low: bfloat16 [2, 2048, 8192], P(None, 'dp', 'tensor')
- down_first_new: float32 [4, 8192, 2048], P(None, 'tensor', 'dp')
- down_second_new: float32 [4, 8192, 2048], P(None, 'tensor', 'dp')
- down_delta: float32 [8192, 2048], P('tensor', 'dp')
- down_outer_new: float32 [8192, 2048], P('tensor', 'dp')
- down_master: float32 [8192, 2048], P('tensor', 'dp')
- down_low: bfloat16 [8192, 2048], P('tensor', 'dp')
- gains_first_new: float32 [4, 2, 2048], replicated
- gains_second_new: float32 [4, 2, 2048], replicated
- gains_delta: float32 [2, 2048], replicated
- gains_outer_new: float32 [2, 2048], replicated
- gains_master: float32 [2, 2048], replicated
- gains_low: bfloat16 [2, 2048], replicated
The draws below stay inside these ranges and needn't reach their ends.
Inputs may be any that keep to these rules, and one draw needn't show every extreme that they name: `seq_ids`: each aligned run of 2048 tokens holds two whole sequences, each one or more tokens long; ids never fall within a run and differ between runs. `block_ids`: A token's block is its position within its sequence divided by 256, rounded down; some run holds a sequence of 2047 tokens. `groups`: each group holds 2 shards.
All inputs are finite; a program needn't handle non-finite values.
Results may differ from the reference program's by a relative error of at most 0.023.
Values may be sent and summed in bfloat16 or wider, within the bound.
A program may use at most 512 MiB of HBM per device.

```python
import math
import jax
import jax.numpy as jnp
from jax import lax

D = 2048
HEADS = 32
HDIM = 64
FF = 8192
TOK_DP = 2048
BLOCK = 256
GROUPS = 4
STEP = 4
HD = 2048
SHARDS = 8
TOKENS = 16384
GTOK = 4096


def layout(key):
    run_count = TOKENS // TOK_DP
    split_at = jax.random.randint(jax.random.fold_in(key, 7), (run_count, 1), 1, TOK_DP)
    forced = jax.random.randint(jax.random.fold_in(key, 13), (), 0, run_count)
    split_at = jnp.where(jnp.arange(run_count, dtype=jnp.int32)[:, None] == forced, 1, split_at)
    places = jnp.arange(TOK_DP, dtype=jnp.int32)[None, :]
    second = (places >= split_at).astype(jnp.int32)
    seq_values = 2 * jnp.arange(run_count, dtype=jnp.int32)[:, None] + second
    offsets = places - second * split_at
    return (seq_values.reshape(TOKENS), (offsets // BLOCK).reshape(TOKENS))


def draw_seq_ids(key, part):
    return layout(key)[0]


def draw_block_ids(key, part):
    return layout(key)[1]


def draw_groups(key, part):
    shuffled = jax.random.permutation(jax.random.fold_in(key, 11), SHARDS)
    return (shuffled % GROUPS).astype(jnp.int32)


def levels(stream_key, shape, cuts, least, largest):
    loudness = 1.0
    for dim, shards_of in cuts:
        steps = jax.random.uniform(jax.random.fold_in(jax.random.fold_in(stream_key, 6), dim), (shards_of,), jnp.float32, least / len(cuts), largest / len(cuts))
        loudness = loudness * jnp.repeat(jnp.exp(steps), shape[dim] // shards_of).reshape((-1,) + (1,) * (len(shape) - 1 - dim))
    return loudness


def normal_values(rng, shape, width, reach, cuts=(), kind=jnp.bfloat16):
    gain = levels(rng, shape, cuts, -0.22, 0.18) if cuts else 1.0
    result = jax.random.normal(rng, shape, jnp.float32) * width * gain
    return jnp.minimum(jnp.maximum(result, -reach), reach).astype(kind)


def setup_inputs(seed: int = 0) -> dict:
    keys = jax.random.split(jax.random.key(seed), 26)
    tokens = normal_values(keys[0], (TOKENS, D), 1.0, 6.0, ((0, 32),))
    cotangent = normal_values(keys[1], (TOKENS, D), 1.0, 6.0, ((0, 32),))
    seq_ids = draw_seq_ids(jax.random.fold_in(keys[25], 71), 0)
    block_ids = draw_block_ids(jax.random.fold_in(keys[25], 71), 0)
    groups = draw_groups(jax.random.fold_in(keys[25], 71), 0)
    qkv_weight = normal_values(keys[5], (3, D, HD), D ** -0.5, 0.125, ((1, 8), (2, 4)), jnp.float32)
    out_weight = normal_values(keys[6], (HD, D), (max(HD // 256, 1)) ** -0.5, 2.0, ((0, 4), (1, 8)), jnp.float32)
    gate_weight = normal_values(keys[7], (2, D, FF), D ** -0.5, 0.125, ((1, 8), (2, 4)), jnp.float32)
    down_weight = normal_values(keys[8], (FF, D), FF ** -0.5, 0.0625, ((0, 4), (1, 8)), jnp.float32)
    norm_gains = jnp.clip(1.0 + 0.1 * jax.random.normal(keys[9], (2, D), jnp.float32), 0.5, 1.5)
    qkv_first = normal_values(keys[10], (GROUPS, 3, D, HD), (0.067 * GTOK ** 0.5), 24.0, ((2, 8), (3, 4)), jnp.float32)
    out_first = normal_values(keys[11], (GROUPS, HD, D), (0.0067 * GTOK ** 0.5), 6.0, ((1, 4), (2, 8)), jnp.float32)
    gate_first = normal_values(keys[12], (GROUPS, 2, D, FF), (0.028 * GTOK ** 0.5), 6.0, ((2, 8), (3, 4)), jnp.float32)
    down_first = normal_values(keys[13], (GROUPS, FF, D), (0.067 * GTOK ** 0.5), 24.0, ((1, 4), (2, 8)), jnp.float32)
    gains_first = normal_values(keys[14], (GROUPS, 2, D), (0.078 * GTOK ** 0.5), 32.0, (), jnp.float32)
    qkv_second = jnp.clip(jnp.exp(math.log(311.296) - 1.3862944 * jax.random.uniform(keys[15], (GROUPS, 3, D, HD), jnp.float32) ** levels(keys[15], (GROUPS, 3, D, HD), ((2, 8), (3, 4)), -0.2, 0.2)), 77.824, 311.296)
    out_second = jnp.clip(jnp.exp(math.log(3.11296) - 1.3862944 * jax.random.uniform(keys[16], (GROUPS, HD, D), jnp.float32) ** levels(keys[16], (GROUPS, HD, D), ((1, 4), (2, 8)), -0.2, 0.2)), 0.77824, 3.11296)
    gate_second = jnp.clip(jnp.exp(math.log(53.248) - 1.3710269 * jax.random.uniform(keys[17], (GROUPS, 2, D, FF), jnp.float32) ** levels(keys[17], (GROUPS, 2, D, FF), ((2, 8), (3, 4)), -0.2, 0.2)), 13.5168, 53.248)
    down_second = jnp.clip(jnp.exp(math.log(311.296) - 1.3862944 * jax.random.uniform(keys[18], (GROUPS, FF, D), jnp.float32) ** levels(keys[18], (GROUPS, FF, D), ((1, 4), (2, 8)), -0.2, 0.2)), 77.824, 311.296)
    gains_second = jnp.clip(jnp.exp(jax.random.uniform(keys[19], (GROUPS, 2, D), jnp.float32, math.log(106.496), math.log(409.6))), 106.496, 409.6)
    qkv_outer = normal_values(keys[20], (3, D, HD), 0.012, 0.1875, ((1, 8), (2, 4)), jnp.float32)
    out_outer = normal_values(keys[21], (HD, D), 0.18, 2.5, ((0, 4), (1, 8)), jnp.float32)
    gate_outer = normal_values(keys[22], (2, D, FF), 0.012, 0.1875, ((1, 8), (2, 4)), jnp.float32)
    down_outer = normal_values(keys[23], (FF, D), 0.006, 0.09375, ((0, 4), (1, 8)), jnp.float32)
    gains_outer = normal_values(keys[24], (2, D), 0.1, 1.5, (), jnp.float32)
    return {"tokens": tokens, "cotangent": cotangent, "seq_ids": seq_ids, "block_ids": block_ids, "groups": groups, "qkv_weight": qkv_weight, "out_weight": out_weight, "gate_weight": gate_weight, "down_weight": down_weight, "norm_gains": norm_gains, "qkv_first": qkv_first, "out_first": out_first, "gate_first": gate_first, "down_first": down_first, "gains_first": gains_first, "qkv_second": qkv_second, "out_second": out_second, "gate_second": gate_second, "down_second": down_second, "gains_second": gains_second, "qkv_outer": qkv_outer, "out_outer": out_outer, "gate_outer": gate_outer, "down_outer": down_outer, "gains_outer": gains_outer}


@jax.custom_vjp
def low(v):
    return lax.optimization_barrier(v.astype(jnp.bfloat16)).astype(jnp.float32)

@jax.custom_vjp
def low_back(v):
    return v

def low_keep(v):
    return (low(v), None)

def low_pass(kept, grad):
    return (grad,)

def back_keep(v):
    return (v, None)

def back_low(kept, grad):
    return (low(grad),)
low.defvjp(low_keep, low_pass)
low_back.defvjp(back_keep, back_low)
norm_eps = 1e-05
rope_base = 130000.0
beta_first = 0.9
beta_second = 0.95
adam_eps = 1e-08
outer_rate = 0.7
outer_beta = 0.9
inner_rates = (0.04, 0.6, 0.04, 0.02, 0.35)
decays = (0.1, 0.1, 0.1, 0.1, 0.0)
highest = lax.Precision.HIGHEST

def rotate(values):
    middle = values.shape[-1] // 2
    return jnp.concatenate([-values[..., middle:], values[..., :middle]], axis=-1)

def tables(seq_part, head_dim):
    length = seq_part.shape[0]
    places = jnp.arange(length, dtype=jnp.int32)
    before = lax.optimization_barrier(jnp.sum((seq_part[None, :] < seq_part[:, None]).astype(jnp.int32), axis=1))
    where_at = (places - before).astype(jnp.float32)
    inverse = rope_base ** (-(jnp.arange(head_dim // 2, dtype=jnp.float32) * 2.0 / head_dim))
    angles = where_at[:, None] * inverse[None, :]
    angles = jnp.concatenate([angles, angles], axis=1)
    return (jnp.cos(angles)[:, None, :], jnp.sin(angles)[:, None, :])

def normed(field_rows, gain_row):
    return field_rows * lax.rsqrt(lax.optimization_barrier(jnp.mean(field_rows * field_rows, axis=-1, keepdims=True)) + norm_eps) * gain_row

def matmul(left_op, right_op):
    return jnp.dot(left_op, right_op, precision=highest, preferred_element_type=jnp.float32)

def attend(queries, keys_all, values_all, seq_part, block_part):
    shard_rows = queries.shape[0]
    block_rows = min(512, shard_rows)
    blocks = shard_rows // block_rows

    def one_block(inputs_one):
        query_block, seq_block, kind_block = inputs_one
        logits = jnp.einsum('qhd,khd->hqk', query_block, keys_all, precision=highest) * HDIM ** (-0.5)
        logits = low_back(logits)
        allowed = (seq_block[:, None] == seq_part[None, :]) & (kind_block[:, None] >= block_part[None, :])
        logits = jnp.where(allowed[None], logits, -jnp.inf)
        softmax_out = low(jax.nn.softmax(logits, axis=-1))
        return jnp.einsum('hqk,khd->qhd', softmax_out, values_all, precision=highest)
    mixture = lax.map(jax.checkpoint(one_block), (queries.reshape((blocks, block_rows) + queries.shape[1:]), seq_part.reshape(blocks, block_rows), block_part.reshape(blocks, block_rows)))
    return mixture.reshape(shard_rows, HEADS * HDIM)

def block_layer(params, field_in, seq_part, block_part):
    qkv_low = low(params[0])
    out_low = low(params[1])
    gate_low = low(params[2])
    down_low = low(params[3])
    gains_all = params[4]
    shard_rows = field_in.shape[0]
    cosine, sine_table = tables(seq_part, HDIM)
    normed_one = low(normed(field_in, gains_all[0]))

    def project(member_id):
        return low_back(matmul(normed_one, qkv_low[member_id])).reshape(shard_rows, HEADS, HDIM)
    query_raw = project(0)
    key_raw = project(1)
    queries = low(query_raw * cosine + rotate(query_raw) * sine_table)
    keys_all = low(key_raw * cosine + rotate(key_raw) * sine_table)
    values_all = low(project(2))
    mixture = low_back(low(attend(queries, keys_all, values_all, seq_part, block_part)))
    residual = field_in + low_back(matmul(mixture, out_low))
    ffn_input = low(normed(residual, gains_all[1]))
    gate_pre = low_back(matmul(ffn_input, gate_low[0]))
    up_pre = low_back(matmul(ffn_input, gate_low[1]))
    hidden = low(jax.nn.silu(gate_pre) * up_pre)
    return residual + matmul(hidden, down_low)

def update(weight, gradient, first_old, second_old, outer_old, step_rate, decay_rate):
    first_new = beta_first * first_old + (1.0 - beta_first) * gradient
    second_new = beta_second * second_old + (1.0 - beta_second) * gradient * gradient
    fix_first = 1.0 - beta_first ** STEP
    fix_second = 1.0 - beta_second ** STEP
    stepped = weight[None] - step_rate * (first_new / fix_first / (jnp.sqrt(second_new / fix_second) + adam_eps) + decay_rate * weight[None])
    change = lax.optimization_barrier(jnp.mean(weight[None] - stepped, axis=0))
    outer_new = outer_beta * outer_old + change
    master = weight - outer_rate * (change + outer_beta * outer_new)
    return (first_new, second_new, change, outer_new, master, master.astype(jnp.bfloat16))

def reference(tokens, cotangent, seq_ids, block_ids, groups, qkv_weight, out_weight, gate_weight, down_weight, norm_gains, qkv_first, out_first, gate_first, down_first, gains_first, qkv_second, out_second, gate_second, down_second, gains_second, qkv_outer, out_outer, gate_outer, down_outer, gains_outer):
    params = (qkv_weight, out_weight, gate_weight, down_weight, norm_gains)
    shards = tokens.shape[0] // TOK_DP
    inputs = (tokens.astype(jnp.float32).reshape(shards, TOK_DP, D), cotangent.astype(jnp.float32).reshape(shards, TOK_DP, D), seq_ids.reshape(shards, TOK_DP), block_ids.reshape(shards, TOK_DP), groups)
    starting = tuple((jnp.zeros((GROUPS,) + weight.shape, jnp.float32) for weight in params))

    def shard_step(totals, inputs_one):
        shard_in, cotan_in, seq_part, block_part, group_id = inputs_one

        def forward(weights_now, values_now):
            return block_layer(weights_now, values_now, seq_part, block_part)
        output, pullback = jax.vjp(forward, params, shard_in)
        weight_grads, shard_grad = pullback(cotan_in)
        chosen = (jnp.arange(GROUPS, dtype=jnp.int32) == group_id).astype(jnp.float32)
        totals = tuple((total_old + chosen.reshape((GROUPS,) + (1,) * member.ndim) * member[None] for total_old, member in zip(totals, weight_grads)))
        return (totals, (output.astype(jnp.bfloat16), shard_grad))
    gradients, (outputs, shard_grads) = lax.scan(shard_step, starting, inputs)
    layer_out = outputs.reshape(tokens.shape[0], D)
    tokens_grad = shard_grads.reshape(tokens.shape[0], D)
    firsts = (qkv_first, out_first, gate_first, down_first, gains_first)
    seconds = (qkv_second, out_second, gate_second, down_second, gains_second)
    outers = (qkv_outer, out_outer, gate_outer, down_outer, gains_outer)
    kinds = [update(params[position], gradients[position], firsts[position], seconds[position], outers[position], inner_rates[position], decays[position]) for position in range(5)]
    qkv_first_new, qkv_second_new, qkv_delta, qkv_outer_new, qkv_master, qkv_low = kinds[0]
    out_first_new, out_second_new, out_delta, out_outer_new, out_master, out_low = kinds[1]
    gate_first_new, gate_second_new, gate_delta, gate_outer_new, gate_master, gate_low = kinds[2]
    down_first_new, down_second_new, down_delta, down_outer_new, down_master, down_low = kinds[3]
    gains_first_new, gains_second_new, gains_delta, gains_outer_new, gains_master, gains_low = kinds[4]
    return (layer_out, tokens_grad, qkv_first_new, qkv_second_new, qkv_delta, qkv_outer_new, qkv_master, qkv_low, out_first_new, out_second_new, out_delta, out_outer_new, out_master, out_low, gate_first_new, gate_second_new, gate_delta, gate_outer_new, gate_master, gate_low, down_first_new, down_second_new, down_delta, down_outer_new, down_master, down_low, gains_first_new, gains_second_new, gains_delta, gains_outer_new, gains_master, gains_low)
```

```python
import functools

import jax
import jax.numpy as jnp
from jax import lax
from jax.experimental import pallas as pl
from jax.experimental.pallas import tpu as pltpu
from jax.sharding import PartitionSpec as P

NT = (((1,), (1,)), ((), ()))
TN = (((0,), (0,)), ((), ()))
NEG = -1e30
LANES = 128


def swap_halves(u):
    lane = lax.broadcasted_iota(jnp.int32, u.shape, 1)
    return jnp.where(lane % 64 < 32, pltpu.roll(u, 96, 1), pltpu.roll(u, 32, 1))


def head_parts(u):
    lane = lax.broadcasted_iota(jnp.int32, u.shape, 1)
    zero = jnp.zeros_like(u)
    return jnp.where(lane < 64, u, zero), jnp.where(lane < 64, zero, u)


def fwd_kernel(tq, tk, info, q_ref, k_ref, v_ref, cos_ref, sin_ref, lo_ref, hi_ref,
               o_ref, qr_ref, kr_ref, vr_ref, lse_ref, q2, v2, m_s, l_s, acc):
    rows = q_ref.shape[0]
    step = 256
    def prep(i, c):
        at = pl.ds(pl.multiple_of(i * step, step), step)
        cos, sin = cos_ref[at, :], sin_ref[at, :]
        q = q_ref[at, :]
        q = (q * cos + swap_halves(q) * sin).astype(jnp.bfloat16) * jnp.bfloat16(0.125)
        k = k_ref[at, :]
        k = (k * cos + swap_halves(k) * sin).astype(jnp.bfloat16)
        v = v_ref[at, :].astype(jnp.bfloat16)
        qr_ref[at, :] = q
        kr_ref[at, :] = k
        vr_ref[at, :] = v
        q2[0, at, :], q2[1, at, :] = head_parts(q)
        v2[0, at, :], v2[1, at, :] = head_parts(v)
        return c
    lax.fori_loop(0, rows // step, prep, 0)

    def q_tile(i, c):
        at = pl.ds(pl.multiple_of(i * tq, tq), tq)
        m_s[...] = jnp.full_like(m_s, -1e29)
        l_s[...] = jnp.zeros_like(l_s)
        acc[...] = jnp.zeros_like(acc)
        first = info[0, i] // tk
        last = (info[3, i] + tk - 1) // tk

        def tile(j, masked):
            ks = pl.multiple_of(j * tk, tk)
            kat = pl.ds(ks, tk)
            k = kr_ref[kat, :]
            if masked:
                key = lax.broadcasted_iota(jnp.int32, (tq, tk), 1) + ks
                ok = (key >= lo_ref[at, :]) & (key < hi_ref[at, :])
            for h in range(2):
                s = lax.dot_general(q2[h, at, :], k, NT, preferred_element_type=jnp.float32)
                if masked:
                    s = jnp.where(ok, s, NEG)
                m_old = m_s[h]
                m_new = jnp.maximum(m_old, jnp.max(s, axis=1, keepdims=True))
                p = jnp.exp(s - m_new[:, :1])
                alpha = jnp.exp(m_old - m_new)
                l_s[h] = alpha * l_s[h] + jnp.sum(p, axis=1, keepdims=True)
                acc[h] = acc[h] * alpha + jnp.dot(
                    p.astype(jnp.bfloat16), v2[h, kat, :], preferred_element_type=jnp.float32)
                m_s[h] = m_new

        def kv_tile(j, c):
            ks = j * tk
            full = (info[1, i] <= ks) & (info[2, i] >= ks + tk)
            @pl.when(full)
            def _():
                tile(j, False)
            @pl.when(jnp.logical_not(full))
            def _():
                tile(j, True)
            return c
        lax.fori_loop(first, last, kv_tile, 0)
        l0, l1 = l_s[0], l_s[1]
        o_ref[at, :] = (acc[0] / l0 + acc[1] / l1).astype(jnp.bfloat16)
        lane = lax.broadcasted_iota(jnp.int32, (tq, LANES), 1)
        lse = jnp.where(lane < 64, m_s[0] + jnp.log(l0), m_s[1] + jnp.log(l1))
        flat = lse.T
        lse_ref[0, 0:1, at] = flat[0:1, :]
        lse_ref[0, 1:2, at] = flat[64:65, :]
        return c
    lax.fori_loop(0, rows // tq, q_tile, 0)


def attn_fwd(info, proj, cos, sin, lo, hi, tq, tk):
    rows, width = proj.shape
    pairs = width // 3 // LANES
    full = lambda p: (0, 0)
    blk = (rows, LANES)
    outs = [jax.ShapeDtypeStruct((rows, pairs * LANES), jnp.bfloat16)] * 4 + [
        jax.ShapeDtypeStruct((pairs, 2, rows), jnp.float32)]
    pair_spec = pl.BlockSpec(blk, lambda p: (0, p))
    area = rows * rows * pairs * 2 * 0.6
    return pl.pallas_call(
        functools.partial(fwd_kernel, tq, tk),
        out_shape=outs,
        grid=(pairs,),
        in_specs=[
            pl.BlockSpec(memory_space=pltpu.SMEM),
            pl.BlockSpec(blk, lambda p: (0, p)),
            pl.BlockSpec(blk, lambda p: (0, p + pairs)),
            pl.BlockSpec(blk, lambda p: (0, p + 2 * pairs)),
            pl.BlockSpec(blk, full), pl.BlockSpec(blk, full),
            pl.BlockSpec((rows, 1), full), pl.BlockSpec((rows, 1), full)],
        out_specs=[pair_spec] * 4 + [pl.BlockSpec((1, 2, rows), lambda p: (p, 0, 0))],
        scratch_shapes=[pltpu.VMEM((2, rows, LANES), jnp.bfloat16), pltpu.VMEM((2, rows, LANES), jnp.bfloat16),
                        pltpu.VMEM((2, tq, LANES), jnp.float32), pltpu.VMEM((2, tq, LANES), jnp.float32),
                        pltpu.VMEM((2, tq, LANES), jnp.float32)],
        compiler_params=pltpu.CompilerParams(vmem_limit_bytes=48 << 20),
        cost_estimate=pl.CostEstimate(flops=int(4 * area * 64), transcendentals=int(area), bytes_accessed=rows * width * 4),
        name="attn_fwd",
    )(info, proj, proj, proj, cos, sin, lo, hi)


def bwd_kernel(tq, tk, info, q_ref, k_ref, v_ref, o_ref, do_ref, lse_ref, cos_ref, sin_ref, lo_ref, hi_ref,
               dq_ref, dk_ref, dv_ref, q2, k2, v2, g2, delta, dq_acc, dk_acc, dv_acc):
    rows = q_ref.shape[0]
    step = 256
    def prep(i, c):
        at = pl.ds(pl.multiple_of(i * step, step), step)
        q2[0, at, :], q2[1, at, :] = head_parts(q_ref[at, :])
        k2[0, at, :], k2[1, at, :] = head_parts(k_ref[at, :])
        v2[0, at, :], v2[1, at, :] = head_parts(v_ref[at, :])
        g = do_ref[at, :]
        g2[0, at, :], g2[1, at, :] = head_parts(g)
        prod = (g.astype(jnp.float32) * o_ref[at, :].astype(jnp.float32)).T
        delta[0:1, at] = jnp.sum(prod[:64], axis=0, keepdims=True)
        delta[1:2, at] = jnp.sum(prod[64:], axis=0, keepdims=True)
        dq_acc[at, :] = jnp.zeros((step, LANES), jnp.float32)
        return c
    lax.fori_loop(0, rows // step, prep, 0)

    def k_tile(j, c):
        ks = pl.multiple_of(j * tk, tk)
        kat = pl.ds(ks, tk)
        dk_acc[...] = jnp.zeros_like(dk_acc)
        dv_acc[...] = jnp.zeros_like(dv_acc)
        first = info[4, j] // tq
        last = (info[5, j] + tq - 1) // tq

        def tile(i, masked):
            at = pl.ds(pl.multiple_of(i * tq, tq), tq)
            if masked:
                key = lax.broadcasted_iota(jnp.int32, (tk, tq), 0) + ks
                ok = (key >= lo_ref[0:1, at]) & (key < hi_ref[0:1, at])
            for h in range(2):
                kh, qh, gh = k2[h, kat, :], q2[h, at, :], g2[h, at, :]
                s = lax.dot_general(kh, qh, NT, preferred_element_type=jnp.float32)
                if masked:
                    s = jnp.where(ok, s, NEG)
                p = jnp.exp(s - lse_ref[0, h:h + 1, at])
                dp = lax.dot_general(v2[h, kat, :], gh, NT, preferred_element_type=jnp.float32)
                ds = (p * (dp - delta[h:h + 1, at])).astype(jnp.bfloat16)
                dv_acc[...] += jnp.dot(p.astype(jnp.bfloat16), gh, preferred_element_type=jnp.float32)
                dk_acc[...] += jnp.dot(ds, qh, preferred_element_type=jnp.float32)
                dq_acc[at, :] += lax.dot_general(ds, kh, TN, preferred_element_type=jnp.float32)

        def q_loop(i, c):
            full = (info[1, i] <= ks) & (info[2, i] >= ks + tk)
            @pl.when(full)
            def _():
                tile(i, False)
            @pl.when(jnp.logical_not(full))
            def _():
                tile(i, True)
            return c
        lax.fori_loop(first, last, q_loop, 0)
        cos, sin = cos_ref[kat, :], sin_ref[kat, :]
        dk = dk_acc[...]
        dk_ref[kat, :] = (dk * cos - swap_halves(dk) * sin).astype(jnp.bfloat16)
        dv_ref[kat, :] = dv_acc[...].astype(jnp.bfloat16)
        return c
    lax.fori_loop(0, rows // tk, k_tile, 0)

    def finish(i, c):
        at = pl.ds(pl.multiple_of(i * step, step), step)
        dq = dq_acc[at, :] * 0.125
        dq_ref[at, :] = (dq * cos_ref[at, :] - swap_halves(dq) * sin_ref[at, :]).astype(jnp.bfloat16)
        return c
    lax.fori_loop(0, rows // step, finish, 0)


def attn_bwd(info, q, k, v, o, do, lse, cos, sin, lo, hi, tq, tk):
    rows, width = q.shape
    pairs = width // LANES
    full = lambda p: (0, 0)
    blk = (rows, LANES)
    pair_spec = pl.BlockSpec(blk, lambda p: (0, p))
    area = rows * rows * pairs * 2 * 0.6
    return pl.pallas_call(
        functools.partial(bwd_kernel, tq, tk),
        out_shape=[jax.ShapeDtypeStruct((rows, width), jnp.bfloat16)] * 3,
        grid=(pairs,),
        in_specs=[pl.BlockSpec(memory_space=pltpu.SMEM)] + [pair_spec] * 5 + [
            pl.BlockSpec((1, 2, rows), lambda p: (p, 0, 0)),
            pl.BlockSpec(blk, full), pl.BlockSpec(blk, full),
            pl.BlockSpec((1, rows), full), pl.BlockSpec((1, rows), full)],
        out_specs=[pair_spec] * 3,
        scratch_shapes=[pltpu.VMEM((2, rows, LANES), jnp.bfloat16)] * 4 + [
            pltpu.VMEM((2, rows), jnp.float32), pltpu.VMEM((rows, LANES), jnp.float32),
            pltpu.VMEM((tk, LANES), jnp.float32), pltpu.VMEM((tk, LANES), jnp.float32)],
        compiler_params=pltpu.CompilerParams(vmem_limit_bytes=48 << 20),
        cost_estimate=pl.CostEstimate(flops=int(10 * area * 64), transcendentals=int(area), bytes_accessed=rows * width * 16),
        name="attn_bwd",
    )(info, q, k, v, o, do, lse, cos, sin, lo, hi)


def layout_of(seq, block, tq, tk):
    rows = seq.shape[0]
    code = seq * 8 + block
    lo = jnp.sum((seq[None, :] < seq[:, None]).astype(jnp.int32), axis=1)
    hi = jnp.sum((code[None, :] <= code[:, None]).astype(jnp.int32), axis=1)
    lt, ht = lo.reshape(-1, tq), hi.reshape(-1, tq)
    start = jnp.arange(rows // tk, dtype=jnp.int32)[:, None] * tk
    qlo = jnp.sum((hi[None, :] <= start).astype(jnp.int32), axis=1)
    qhi = jnp.sum((lo[None, :] < start + tk).astype(jnp.int32), axis=1)
    info = jnp.stack([lt.min(1), lt.max(1), ht.min(1), ht.max(1), qlo, qhi]) if tq == tk else None
    return lo, hi, info


def rope_tables(lo, base=130000.0):
    rows = lo.shape[0]
    where_at = (jnp.arange(rows, dtype=jnp.int32) - lo).astype(jnp.float32)
    inverse = base ** (-(jnp.arange(32, dtype=jnp.float32) * 2.0 / 64))
    ang = where_at[:, None] * inverse[None, :]
    cos, sin = jnp.cos(ang), jnp.sin(ang)
    return jnp.concatenate([cos] * 4, axis=1), jnp.concatenate([-sin, sin, -sin, sin], axis=1)


HDIM = 64
GROUPS = 4
STEP = 4

norm_eps = 1e-05
beta_first = 0.9
beta_second = 0.95
adam_eps = 1e-08
outer_rate = 0.7
outer_beta = 0.9
inner_rates = (0.04, 0.6, 0.04, 0.02, 0.35)
decays = (0.1, 0.1, 0.1, 0.1, 0.0)
fix_first = 1.0 - beta_first**STEP
fix_second = 1.0 - beta_second**STEP
TILE = 512


def normed(field_rows, gain_row):
    factor = lax.rsqrt(jnp.mean(field_rows * field_rows, axis=-1, keepdims=True) + norm_eps)
    scaled = field_rows * factor
    return ((scaled * gain_row).astype(jnp.bfloat16), scaled, factor)


def norm_back(upstream, scaled, factor, gain_row):
    inside = upstream * gain_row
    return factor * (inside - scaled * jnp.mean(inside * scaled, axis=-1, keepdims=True))


def update(weight, gradient, first_old, second_old, outer_old, step_rate, decay_rate):
    first_new = beta_first * first_old + (1.0 - beta_first) * gradient
    second_new = beta_second * second_old + (1.0 - beta_second) * gradient * gradient
    ratio = first_new / fix_first / (jnp.sqrt(second_new / fix_second) + adam_eps)
    change = step_rate * (jnp.mean(ratio, axis=0) + decay_rate * weight)
    outer_new = outer_beta * outer_old + change
    master = weight - outer_rate * (change + outer_beta * outer_new)
    return [first_new, second_new, change, outer_new, master, master.astype(jnp.bfloat16)]


def opt_kernel(per, turned, rate, decay, order, *refs):
    (recv, first, second, weight, outer), (first_new, second_new, delta, outer_new, master, low) = refs[:5], refs[-6:]
    rows, cols = weight.shape[-2:]
    step_r, step_c = min(rows, 16), min(cols, 256)
    if turned:
        step_r, step_c = min(rows, 128), min(cols, 128)
    lead = (0,) * (len(weight.shape) - 2)

    def chunk(i, carry):
        r = pl.multiple_of((i // (cols // step_c)) * step_r, step_r)
        c = pl.multiple_of((i % (cols // step_c)) * step_c, step_c)
        at = (pl.ds(r, step_r), pl.ds(c, step_c))
        w = weight[lead + at]
        total = jnp.zeros_like(w)
        for g in range(GROUPS):
            grad = None
            for j in range(per):
                source = order[g * per + j]
                if turned:
                    part = recv[source, pl.ds(c, step_c), pl.ds(r, step_r)].astype(jnp.float32)
                else:
                    part = recv[(source,) + at].astype(jnp.float32)
                grad = part if grad is None else grad + part
            if turned:
                grad = grad.T
            m = beta_first * first[(g,) + lead + at] + (1.0 - beta_first) * grad
            v = beta_second * second[(g,) + lead + at] + (1.0 - beta_second) * grad * grad
            first_new[(g,) + lead + at] = m
            second_new[(g,) + lead + at] = v
            total = total + m / (jnp.sqrt(v * (1.0 / fix_second)) + adam_eps)
        change = rate * (total * (1.0 / (fix_first * GROUPS)) + decay * w)
        moved = outer_beta * outer[lead + at] + change
        fresh = w - outer_rate * (change + outer_beta * moved)
        delta[lead + at] = change
        outer_new[lead + at] = moved
        master[lead + at] = fresh
        low[lead + at] = fresh.astype(jnp.bfloat16)
        return carry

    lax.fori_loop(0, (rows // step_r) * (cols // step_c), chunk, 0)


def optimize(order, recv, weight, first, second, outer, position, turned=False, member=None, before=None):
    sources = recv.shape[0]
    stacked = weight.ndim == 3
    rows, cols = weight.shape[-2:]
    members = weight.shape[0] if stacked and member is None else 1
    base = member or 0
    area = 65536
    if turned:
        br, bc = max(128, min(rows, area // cols)), cols
    else:
        br, bc = max(16, min(rows, area // cols)), cols
    blocks = rows // br
    lead = (1,) if stacked else ()

    def pick(m):
        return (base + m,) if stacked else ()

    if turned:
        recv_spec = pl.BlockSpec((sources, bc, br), lambda m, i: (0, 0, i))
    else:
        recv_spec = pl.BlockSpec((sources, br, bc), lambda m, i: (0, i, m))
    one = pl.BlockSpec(lead + (br, bc), lambda m, i: pick(m) + (i, 0))
    many = pl.BlockSpec((GROUPS,) + lead + (br, bc), lambda m, i: (0,) + pick(m) + (i, 0))
    f32 = jnp.float32
    outs = [
        jax.ShapeDtypeStruct(first.shape, f32),
        jax.ShapeDtypeStruct(first.shape, f32),
        jax.ShapeDtypeStruct(weight.shape, f32),
        jax.ShapeDtypeStruct(weight.shape, f32),
        jax.ShapeDtypeStruct(weight.shape, f32),
        jax.ShapeDtypeStruct(weight.shape, jnp.bfloat16),
    ]
    operands = [order, recv, first, second, weight, outer]
    specs = [pl.BlockSpec(memory_space=pltpu.SMEM), recv_spec, many, many, one, one]
    aliases = {}
    if before is not None:
        aliases = {len(operands) + k: k for k in range(6)}
        operands += list(before)
        specs += [pl.BlockSpec(memory_space=pl.ANY)] * 6
    count = members * rows * cols
    return pl.pallas_call(
        functools.partial(
            opt_kernel, sources // GROUPS, turned, inner_rates[position], decays[position]
        ),
        out_shape=outs,
        grid=(members, blocks),
        in_specs=specs,
        out_specs=[many, many, one, one, one, one],
        input_output_aliases=aliases,
        compiler_params=pltpu.CompilerParams(vmem_limit_bytes=40 << 20),
        cost_estimate=pl.CostEstimate(
            flops=60 * count, transcendentals=8 * count, bytes_accessed=(86 + 2 * sources) * count
        ),
        name="optimize",
    )(*operands)


def dot(left, right):
    return jnp.dot(left, right, preferred_element_type=jnp.float32)


def dot_cols(left, right):
    return lax.dot_general(left, right, (((1,), (1,)), ((), ())), preferred_element_type=jnp.float32)


def dot_rows(left, right):
    return lax.dot_general(left, right, (((0,), (0,)), ((), ())), preferred_element_type=jnp.float32)


def gather_rows(part, axis):
    return lax.all_gather(part, axis, axis=0, tiled=True)


def spread_rows(part):
    count = lax.axis_size("tensor")
    copies = jnp.broadcast_to(part[None], (count,) + part.shape)
    return lax.all_to_all(copies, "tensor", split_axis=0, concat_axis=0).reshape((-1,) + part.shape[1:])


def sum_rows(part):
    count = lax.axis_size("tensor")
    blocks = part.reshape((count, part.shape[0] // count) + part.shape[1:])
    return jnp.sum(lax.all_to_all(blocks, "tensor", split_axis=0, concat_axis=0).astype(jnp.float32), axis=0)


def scatter_rows(part):
    return lax.psum_scatter(part, "tensor", scatter_dimension=0, tiled=True).astype(jnp.float32)


def to_owners(grad):
    count = lax.axis_size("dp")
    blocks = grad.astype(jnp.bfloat16).reshape((count, grad.shape[0] // count) + grad.shape[1:])
    return lax.all_to_all(blocks, "dp", split_axis=0, concat_axis=0)


def on_device(
    tokens,
    cotangent,
    seq_ids,
    block_ids,
    groups,
    qkv_weight,
    out_weight,
    gate_weight,
    down_weight,
    norm_gains,
    qkv_first,
    out_first,
    gate_first,
    down_first,
    gains_first,
    qkv_second,
    out_second,
    gate_second,
    down_second,
    gains_second,
    qkv_outer,
    out_outer,
    gate_outer,
    down_outer,
    gains_outer,
):
    bf16 = jnp.bfloat16
    field_in = tokens.astype(jnp.float32)
    normed_one, scaled_one, factor_one = normed(field_in, norm_gains[0])
    normed_all = spread_rows(normed_one)
    qkv_full = gather_rows(
        jnp.concatenate([qkv_weight[m].astype(bf16) for m in range(3)], axis=1), "dp"
    )
    out_full = gather_rows(out_weight.T.astype(bf16), "dp")
    wide = gate_weight.shape[2]
    gate_full = gather_rows(gate_weight[0].astype(bf16), "dp")
    up_full = gather_rows(gate_weight[1].astype(bf16), "dp")
    down_full = gather_rows(down_weight.T.astype(bf16), "dp")
    cotan_all = spread_rows(lax.optimization_barrier((cotangent, normed_all))[0])

    lo, hi, info = layout_of(seq_ids, block_ids, TILE, TILE)
    cosine, sine_table = rope_tables(lo)
    order = jnp.argsort(groups, stable=True).astype(jnp.int32)

    projected = dot(normed_all, qkv_full)
    mixed_all, queries, keys_all, values_all, logsums = attn_fwd(
        info, projected, cosine, sine_table, lo[:, None], hi[:, None], TILE, TILE
    )
    attn_rows = sum_rows(dot_cols(mixed_all, out_full).astype(bf16))
    residual = field_in + attn_rows
    normed_two, scaled_two, factor_two = normed(residual, norm_gains[1])
    ffn_input = gather_rows(normed_two, "tensor")
    gate_pre = dot(ffn_input, gate_full)
    up_pre = dot(ffn_input, up_full)
    sigmoid_gate = jax.nn.sigmoid(gate_pre)
    swish = gate_pre * sigmoid_gate
    hidden = (swish * up_pre).astype(bf16)
    down_recv = to_owners(dot_rows(cotan_all, hidden))
    ffn_part = scatter_rows(dot_cols(hidden, down_full).astype(bf16))
    layer_out = (residual + ffn_part).astype(bf16)
    hidden_grad = dot(cotan_all, down_full)
    gate_grad_low = (
        hidden_grad * up_pre * sigmoid_gate * (1.0 + gate_pre * (1.0 - sigmoid_gate))
    ).astype(bf16)
    up_grad_low = (hidden_grad * swish).astype(bf16)
    ffn_back_rows = scatter_rows(
        (dot_cols(gate_grad_low, gate_full) + dot_cols(up_grad_low, up_full)).astype(bf16)
    )
    gate_recv = to_owners(dot_rows(ffn_input, gate_grad_low))
    up_recv = to_owners(dot_rows(ffn_input, up_grad_low))
    cotan_rows = cotangent.astype(jnp.float32)
    resid_grad = cotan_rows + norm_back(ffn_back_rows, scaled_two, factor_two, norm_gains[1])
    gain_two = jnp.sum(ffn_back_rows * scaled_two, axis=0)
    resid_all = gather_rows(resid_grad.astype(bf16), "tensor")
    mixed_grad = dot(resid_all, out_full).astype(bf16)
    out_recv = to_owners(dot_rows(resid_all, mixed_all))
    raw_grads = attn_bwd(
        info, queries, keys_all, values_all, mixed_all, mixed_grad, logsums,
        cosine, sine_table, lo[None], hi[None], TILE, TILE,
    )
    raw_all = jnp.concatenate(raw_grads, axis=1)
    in_grad_rows = scatter_rows(dot_cols(raw_all, qkv_full).astype(bf16))
    qkv_recv = to_owners(dot_rows(normed_all, raw_all))
    tokens_grad = resid_grad + norm_back(in_grad_rows, scaled_one, factor_one, norm_gains[0])
    gain_one = jnp.sum(in_grad_rows * scaled_one, axis=0)
    own_group = (jnp.arange(GROUPS, dtype=jnp.int32) == groups[lax.axis_index("dp")]).astype(
        jnp.float32
    )
    gain_slots = own_group[:, None, None] * jnp.stack([gain_one, gain_two])[None]
    gain_grad = lax.psum(gain_slots, ("dp", "tensor"))

    down_new = optimize(
        order, down_recv, down_weight, down_first, down_second, down_outer, 3, turned=True
    )
    gate_half = optimize(
        order, gate_recv, gate_weight, gate_first, gate_second, gate_outer, 2, member=0
    )
    gate_new = optimize(
        order, up_recv, gate_weight, gate_first, gate_second, gate_outer, 2, member=1, before=gate_half
    )
    out_new = optimize(
        order, out_recv, out_weight, out_first, out_second, out_outer, 1, turned=True
    )
    qkv_new = optimize(order, qkv_recv, qkv_weight, qkv_first, qkv_second, qkv_outer, 0)
    gains_new = update(
        norm_gains, gain_grad, gains_first, gains_second, gains_outer, inner_rates[4], decays[4]
    )
    return (layer_out, tokens_grad, *qkv_new, *out_new, *gate_new, *down_new, *gains_new)


def solution(mesh):
    in_specs = (
        P(("dp", "tensor"), None),
        P(("dp", "tensor"), None),
        P("dp"),
        P("dp"),
        P(),
        P(None, "dp", "tensor"),
        P("tensor", "dp"),
        P(None, "dp", "tensor"),
        P("tensor", "dp"),
        P(),
        P(None, None, "dp", "tensor"),
        P(None, "tensor", "dp"),
        P(None, None, "dp", "tensor"),
        P(None, "tensor", "dp"),
        P(),
        P(None, None, "dp", "tensor"),
        P(None, "tensor", "dp"),
        P(None, None, "dp", "tensor"),
        P(None, "tensor", "dp"),
        P(),
        P(None, "dp", "tensor"),
        P("tensor", "dp"),
        P(None, "dp", "tensor"),
        P("tensor", "dp"),
        P(),
    )
    out_specs = (
        P(("dp", "tensor"), None),
        P(("dp", "tensor"), None),
        P(None, None, "dp", "tensor"),
        P(None, None, "dp", "tensor"),
        P(None, "dp", "tensor"),
        P(None, "dp", "tensor"),
        P(None, "dp", "tensor"),
        P(None, "dp", "tensor"),
        P(None, "tensor", "dp"),
        P(None, "tensor", "dp"),
        P("tensor", "dp"),
        P("tensor", "dp"),
        P("tensor", "dp"),
        P("tensor", "dp"),
        P(None, None, "dp", "tensor"),
        P(None, None, "dp", "tensor"),
        P(None, "dp", "tensor"),
        P(None, "dp", "tensor"),
        P(None, "dp", "tensor"),
        P(None, "dp", "tensor"),
        P(None, "tensor", "dp"),
        P(None, "tensor", "dp"),
        P("tensor", "dp"),
        P("tensor", "dp"),
        P("tensor", "dp"),
        P("tensor", "dp"),
        P(),
        P(),
        P(),
        P(),
        P(),
        P(),
    )
    return jax.shard_map(
        on_device, mesh=mesh, in_specs=in_specs, out_specs=out_specs, check_vma=False
    )
```

```python
import functools

import jax
import jax.numpy as jnp
from jax import lax
from jax.experimental import pallas as pl
from jax.experimental.pallas import tpu as pltpu
from jax.sharding import PartitionSpec as P

NT = (((1,), (1,)), ((), ()))
TN = (((0,), (0,)), ((), ()))
NEG = -1e30
LANES = 128


def swap_halves(u):
    lane = lax.broadcasted_iota(jnp.int32, u.shape, 1)
    return jnp.where(lane % 64 < 32, pltpu.roll(u, 96, 1), pltpu.roll(u, 32, 1))


def head_parts(u):
    lane = lax.broadcasted_iota(jnp.int32, u.shape, 1)
    zero = jnp.zeros_like(u)
    return jnp.where(lane < 64, u, zero), jnp.where(lane < 64, zero, u)


def fwd_kernel(tq, tk, info, q_ref, k_ref, v_ref, cos_ref, sin_ref, lo_ref, hi_ref,
               o_ref, qr_ref, kr_ref, vr_ref, lse_ref, q2, v2, m_s, l_s, acc):
    rows = q_ref.shape[0]
    step = 256
    def prep(i, c):
        at = pl.ds(pl.multiple_of(i * step, step), step)
        cos, sin = cos_ref[at, :], sin_ref[at, :]
        q = q_ref[at, :]
        q = (q * cos + swap_halves(q) * sin).astype(jnp.bfloat16) * jnp.bfloat16(0.125)
        k = k_ref[at, :]
        k = (k * cos + swap_halves(k) * sin).astype(jnp.bfloat16)
        v = v_ref[at, :].astype(jnp.bfloat16)
        qr_ref[at, :] = q
        kr_ref[at, :] = k
        vr_ref[at, :] = v
        q2[0, at, :], q2[1, at, :] = head_parts(q)
        v2[0, at, :], v2[1, at, :] = head_parts(v)
        return c
    lax.fori_loop(0, rows // step, prep, 0)

    def q_tile(i, c):
        at = pl.ds(pl.multiple_of(i * tq, tq), tq)
        m_s[...] = jnp.full_like(m_s, -1e29)
        l_s[...] = jnp.zeros_like(l_s)
        acc[...] = jnp.zeros_like(acc)
        first = info[0, i] // tk
        last = (info[3, i] + tk - 1) // tk

        def tile(j, masked):
            ks = pl.multiple_of(j * tk, tk)
            kat = pl.ds(ks, tk)
            k = kr_ref[kat, :]
            if masked:
                key = lax.broadcasted_iota(jnp.int32, (tq, tk), 1) + ks
                ok = (key >= lo_ref[at, :]) & (key < hi_ref[at, :])
            for h in range(2):
                s = lax.dot_general(q2[h, at, :], k, NT, preferred_element_type=jnp.float32)
                if masked:
                    s = jnp.where(ok, s, NEG)
                m_old = m_s[h]
                m_new = jnp.maximum(m_old, jnp.max(s, axis=1, keepdims=True))
                p = jnp.exp(s - m_new[:, :1])
                alpha = jnp.exp(m_old - m_new)
                l_s[h] = alpha * l_s[h] + jnp.sum(p, axis=1, keepdims=True)
                acc[h] = acc[h] * alpha + jnp.dot(
                    p.astype(jnp.bfloat16), v2[h, kat, :], preferred_element_type=jnp.float32)
                m_s[h] = m_new

        def kv_tile(j, c):
            ks = j * tk
            full = (info[1, i] <= ks) & (info[2, i] >= ks + tk)
            @pl.when(full)
            def _():
                tile(j, False)
            @pl.when(jnp.logical_not(full))
            def _():
                tile(j, True)
            return c
        lax.fori_loop(first, last, kv_tile, 0)
        l0, l1 = l_s[0], l_s[1]
        o_ref[at, :] = (acc[0] / l0 + acc[1] / l1).astype(jnp.bfloat16)
        lane = lax.broadcasted_iota(jnp.int32, (tq, LANES), 1)
        lse = jnp.where(lane < 64, m_s[0] + jnp.log(l0), m_s[1] + jnp.log(l1))
        flat = lse.T
        lse_ref[0, 0:1, at] = flat[0:1, :]
        lse_ref[0, 1:2, at] = flat[64:65, :]
        return c
    lax.fori_loop(0, rows // tq, q_tile, 0)


def attn_fwd(info, proj, cos, sin, lo, hi, tq, tk):
    rows, width = proj.shape
    pairs = width // 3 // LANES
    full = lambda p: (0, 0)
    blk = (rows, LANES)
    outs = [jax.ShapeDtypeStruct((rows, pairs * LANES), jnp.bfloat16)] * 4 + [
        jax.ShapeDtypeStruct((pairs, 2, rows), jnp.float32)]
    pair_spec = pl.BlockSpec(blk, lambda p: (0, p))
    area = rows * rows * pairs * 2 * 0.6
    return pl.pallas_call(
        functools.partial(fwd_kernel, tq, tk),
        out_shape=outs,
        grid=(pairs,),
        in_specs=[
            pl.BlockSpec(memory_space=pltpu.SMEM),
            pl.BlockSpec(blk, lambda p: (0, p)),
            pl.BlockSpec(blk, lambda p: (0, p + pairs)),
            pl.BlockSpec(blk, lambda p: (0, p + 2 * pairs)),
            pl.BlockSpec(blk, full), pl.BlockSpec(blk, full),
            pl.BlockSpec((rows, 1), full), pl.BlockSpec((rows, 1), full)],
        out_specs=[pair_spec] * 4 + [pl.BlockSpec((1, 2, rows), lambda p: (p, 0, 0))],
        scratch_shapes=[pltpu.VMEM((2, rows, LANES), jnp.bfloat16), pltpu.VMEM((2, rows, LANES), jnp.bfloat16),
                        pltpu.VMEM((2, tq, LANES), jnp.float32), pltpu.VMEM((2, tq, LANES), jnp.float32),
                        pltpu.VMEM((2, tq, LANES), jnp.float32)],
        compiler_params=pltpu.CompilerParams(vmem_limit_bytes=48 << 20),
        cost_estimate=pl.CostEstimate(flops=int(4 * area * 64), transcendentals=int(area), bytes_accessed=rows * width * 4),
        name="attn_fwd",
    )(info, proj, proj, proj, cos, sin, lo, hi)


def bwd_kernel(tq, tk, info, q_ref, k_ref, v_ref, o_ref, do_ref, lse_ref, cos_ref, sin_ref, lo_ref, hi_ref,
               dq_ref, dk_ref, dv_ref, q2, k2, v2, g2, delta, dq_acc, dk_acc, dv_acc):
    rows = q_ref.shape[0]
    step = 256
    def prep(i, c):
        at = pl.ds(pl.multiple_of(i * step, step), step)
        q2[0, at, :], q2[1, at, :] = head_parts(q_ref[at, :])
        k2[0, at, :], k2[1, at, :] = head_parts(k_ref[at, :])
        v2[0, at, :], v2[1, at, :] = head_parts(v_ref[at, :])
        g = do_ref[at, :]
        g2[0, at, :], g2[1, at, :] = head_parts(g)
        prod = (g.astype(jnp.float32) * o_ref[at, :].astype(jnp.float32)).T
        delta[0:1, at] = jnp.sum(prod[:64], axis=0, keepdims=True)
        delta[1:2, at] = jnp.sum(prod[64:], axis=0, keepdims=True)
        dq_acc[at, :] = jnp.zeros((step, LANES), jnp.float32)
        return c
    lax.fori_loop(0, rows // step, prep, 0)

    def k_tile(j, c):
        ks = pl.multiple_of(j * tk, tk)
        kat = pl.ds(ks, tk)
        dk_acc[...] = jnp.zeros_like(dk_acc)
        dv_acc[...] = jnp.zeros_like(dv_acc)
        first = info[4, j] // tq
        last = (info[5, j] + tq - 1) // tq

        def tile(i, masked):
            at = pl.ds(pl.multiple_of(i * tq, tq), tq)
            if masked:
                key = lax.broadcasted_iota(jnp.int32, (tk, tq), 0) + ks
                ok = (key >= lo_ref[0:1, at]) & (key < hi_ref[0:1, at])
            for h in range(2):
                kh, qh, gh = k2[h, kat, :], q2[h, at, :], g2[h, at, :]
                s = lax.dot_general(kh, qh, NT, preferred_element_type=jnp.float32)
                if masked:
                    s = jnp.where(ok, s, NEG)
                p = jnp.exp(s - lse_ref[0, h:h + 1, at])
                dp = lax.dot_general(v2[h, kat, :], gh, NT, preferred_element_type=jnp.float32)
                ds = (p * (dp - delta[h:h + 1, at])).astype(jnp.bfloat16)
                dv_acc[...] += jnp.dot(p.astype(jnp.bfloat16), gh, preferred_element_type=jnp.float32)
                dk_acc[...] += jnp.dot(ds, qh, preferred_element_type=jnp.float32)
                dq_acc[at, :] += lax.dot_general(ds, kh, TN, preferred_element_type=jnp.float32)

        def q_loop(i, c):
            full = (info[1, i] <= ks) & (info[2, i] >= ks + tk)
            @pl.when(full)
            def _():
                tile(i, False)
            @pl.when(jnp.logical_not(full))
            def _():
                tile(i, True)
            return c
        lax.fori_loop(first, last, q_loop, 0)
        cos, sin = cos_ref[kat, :], sin_ref[kat, :]
        dk = dk_acc[...]
        dk_ref[kat, :] = (dk * cos - swap_halves(dk) * sin).astype(jnp.bfloat16)
        dv_ref[kat, :] = dv_acc[...].astype(jnp.bfloat16)
        return c
    lax.fori_loop(0, rows // tk, k_tile, 0)

    def finish(i, c):
        at = pl.ds(pl.multiple_of(i * step, step), step)
        dq = dq_acc[at, :] * 0.125
        dq_ref[at, :] = (dq * cos_ref[at, :] - swap_halves(dq) * sin_ref[at, :]).astype(jnp.bfloat16)
        return c
    lax.fori_loop(0, rows // step, finish, 0)


def attn_bwd(info, q, k, v, o, do, lse, cos, sin, lo, hi, tq, tk):
    rows, width = q.shape
    pairs = width // LANES
    full = lambda p: (0, 0)
    blk = (rows, LANES)
    pair_spec = pl.BlockSpec(blk, lambda p: (0, p))
    area = rows * rows * pairs * 2 * 0.6
    return pl.pallas_call(
        functools.partial(bwd_kernel, tq, tk),
        out_shape=[jax.ShapeDtypeStruct((rows, width), jnp.bfloat16)] * 3,
        grid=(pairs,),
        in_specs=[pl.BlockSpec(memory_space=pltpu.SMEM)] + [pair_spec] * 5 + [
            pl.BlockSpec((1, 2, rows), lambda p: (p, 0, 0)),
            pl.BlockSpec(blk, full), pl.BlockSpec(blk, full),
            pl.BlockSpec((1, rows), full), pl.BlockSpec((1, rows), full)],
        out_specs=[pair_spec] * 3,
        scratch_shapes=[pltpu.VMEM((2, rows, LANES), jnp.bfloat16)] * 4 + [
            pltpu.VMEM((2, rows), jnp.float32), pltpu.VMEM((rows, LANES), jnp.float32),
            pltpu.VMEM((tk, LANES), jnp.float32), pltpu.VMEM((tk, LANES), jnp.float32)],
        compiler_params=pltpu.CompilerParams(vmem_limit_bytes=48 << 20),
        cost_estimate=pl.CostEstimate(flops=int(10 * area * 64), transcendentals=int(area), bytes_accessed=rows * width * 16),
        name="attn_bwd",
    )(info, q, k, v, o, do, lse, cos, sin, lo, hi)


def layout_of(seq, block, tq, tk):
    rows = seq.shape[0]
    code = seq * 8 + block
    lo = jnp.sum((seq[None, :] < seq[:, None]).astype(jnp.int32), axis=1)
    hi = jnp.sum((code[None, :] <= code[:, None]).astype(jnp.int32), axis=1)
    lt, ht = lo.reshape(-1, tq), hi.reshape(-1, tq)
    start = jnp.arange(rows // tk, dtype=jnp.int32)[:, None] * tk
    qlo = jnp.sum((hi[None, :] <= start).astype(jnp.int32), axis=1)
    qhi = jnp.sum((lo[None, :] < start + tk).astype(jnp.int32), axis=1)
    info = jnp.stack([lt.min(1), lt.max(1), ht.min(1), ht.max(1), qlo, qhi]) if tq == tk else None
    return lo, hi, info


def rope_tables(lo, base=130000.0):
    rows = lo.shape[0]
    where_at = (jnp.arange(rows, dtype=jnp.int32) - lo).astype(jnp.float32)
    inverse = base ** (-(jnp.arange(32, dtype=jnp.float32) * 2.0 / 64))
    ang = where_at[:, None] * inverse[None, :]
    cos, sin = jnp.cos(ang), jnp.sin(ang)
    return jnp.concatenate([cos] * 4, axis=1), jnp.concatenate([-sin, sin, -sin, sin], axis=1)


GROUPS = 4
STEP = 4

norm_eps = 1e-05
beta_first = 0.9
beta_second = 0.95
adam_eps = 1e-08
outer_rate = 0.7
outer_beta = 0.9
inner_rates = (0.04, 0.6, 0.04, 0.02, 0.35)
decays = (0.1, 0.1, 0.1, 0.1, 0.0)
fix_first = 1.0 - beta_first**STEP
fix_second = 1.0 - beta_second**STEP
TILE = 512


def normed(field_rows, gain_row):
    factor = lax.rsqrt(jnp.mean(field_rows * field_rows, axis=-1, keepdims=True) + norm_eps)
    scaled = field_rows * factor
    return ((scaled * gain_row).astype(jnp.bfloat16), scaled, factor)


def norm_back(upstream, scaled, factor, gain_row):
    inside = upstream * gain_row
    return factor * (inside - scaled * jnp.mean(inside * scaled, axis=-1, keepdims=True))


def update(weight, gradient, first_old, second_old, outer_old, step_rate, decay_rate):
    first_new = beta_first * first_old + (1.0 - beta_first) * gradient
    second_new = beta_second * second_old + (1.0 - beta_second) * gradient * gradient
    ratio = first_new / fix_first / (jnp.sqrt(second_new / fix_second) + adam_eps)
    change = step_rate * (jnp.mean(ratio, axis=0) + decay_rate * weight)
    outer_new = outer_beta * outer_old + change
    master = weight - outer_rate * (change + outer_beta * outer_new)
    return [first_new, second_new, change, outer_new, master, master.astype(jnp.bfloat16)]


def opt_kernel(per, turned, rate, decay, order, *refs):
    (recv, first, second, weight, outer), (first_new, second_new, delta, outer_new, master, low) = refs[:5], refs[-6:]
    rows, cols = weight.shape[-2:]
    step_r, step_c = min(rows, 16), min(cols, 256)
    if turned:
        step_r, step_c = min(rows, 128), min(cols, 128)
    lead = (0,) * (len(weight.shape) - 2)

    def chunk(i, carry):
        r = pl.multiple_of((i // (cols // step_c)) * step_r, step_r)
        c = pl.multiple_of((i % (cols // step_c)) * step_c, step_c)
        at = (pl.ds(r, step_r), pl.ds(c, step_c))
        w = weight[lead + at]
        total = jnp.zeros_like(w)
        for g in range(GROUPS):
            grad = None
            for j in range(per):
                source = order[g * per + j]
                if turned:
                    part = recv[source, pl.ds(c, step_c), pl.ds(r, step_r)].astype(jnp.float32)
                else:
                    part = recv[(source,) + at].astype(jnp.float32)
                grad = part if grad is None else grad + part
            if turned:
                grad = grad.T
            m = beta_first * first[(g,) + lead + at] + (1.0 - beta_first) * grad
            v = beta_second * second[(g,) + lead + at] + (1.0 - beta_second) * grad * grad
            first_new[(g,) + lead + at] = m
            second_new[(g,) + lead + at] = v
            total = total + m / (jnp.sqrt(v * (1.0 / fix_second)) + adam_eps)
        change = rate * (total * (1.0 / (fix_first * GROUPS)) + decay * w)
        moved = outer_beta * outer[lead + at] + change
        fresh = w - outer_rate * (change + outer_beta * moved)
        delta[lead + at] = change
        outer_new[lead + at] = moved
        master[lead + at] = fresh
        low[lead + at] = fresh.astype(jnp.bfloat16)
        return carry

    lax.fori_loop(0, (rows // step_r) * (cols // step_c), chunk, 0)


def optimize(order, recv, weight, first, second, outer, position, turned=False, member=None, before=None):
    sources = recv.shape[0]
    stacked = weight.ndim == 3
    rows, cols = weight.shape[-2:]
    members = weight.shape[0] if stacked and member is None else 1
    base = member or 0
    area = 65536
    if turned:
        br, bc = max(128, min(rows, area // cols)), cols
    else:
        br, bc = max(16, min(rows, area // cols)), cols
    blocks = rows // br
    lead = (1,) if stacked else ()

    def pick(m):
        return (base + m,) if stacked else ()

    if turned:
        recv_spec = pl.BlockSpec((sources, bc, br), lambda m, i: (0, 0, i))
    else:
        recv_spec = pl.BlockSpec((sources, br, bc), lambda m, i: (0, i, m))
    one = pl.BlockSpec(lead + (br, bc), lambda m, i: pick(m) + (i, 0))
    many = pl.BlockSpec((GROUPS,) + lead + (br, bc), lambda m, i: (0,) + pick(m) + (i, 0))
    f32 = jnp.float32
    outs = [
        jax.ShapeDtypeStruct(first.shape, f32),
        jax.ShapeDtypeStruct(first.shape, f32),
        jax.ShapeDtypeStruct(weight.shape, f32),
        jax.ShapeDtypeStruct(weight.shape, f32),
        jax.ShapeDtypeStruct(weight.shape, f32),
        jax.ShapeDtypeStruct(weight.shape, jnp.bfloat16),
    ]
    operands = [order, recv, first, second, weight, outer]
    specs = [pl.BlockSpec(memory_space=pltpu.SMEM), recv_spec, many, many, one, one]
    aliases = {}
    if before is not None:
        aliases = {len(operands) + k: k for k in range(6)}
        operands += list(before)
        specs += [pl.BlockSpec(memory_space=pl.ANY)] * 6
    count = members * rows * cols
    return pl.pallas_call(
        functools.partial(
            opt_kernel, sources // GROUPS, turned, inner_rates[position], decays[position]
        ),
        out_shape=outs,
        grid=(members, blocks),
        in_specs=specs,
        out_specs=[many, many, one, one, one, one],
        input_output_aliases=aliases,
        compiler_params=pltpu.CompilerParams(vmem_limit_bytes=40 << 20),
        cost_estimate=pl.CostEstimate(
            flops=60 * count, transcendentals=8 * count, bytes_accessed=(86 + 2 * sources) * count
        ),
        name="optimize",
    )(*operands)


def dot(left, right):
    return jnp.dot(left, right, preferred_element_type=jnp.float32)


def dot_cols(left, right):
    return lax.dot_general(left, right, (((1,), (1,)), ((), ())), preferred_element_type=jnp.float32)


def dot_rows(left, right):
    return lax.dot_general(left, right, (((0,), (0,)), ((), ())), preferred_element_type=jnp.float32)


def after(value, *others):
    return lax.optimization_barrier((value,) + others)[0]


def tick_kernel(source, mark):
    mark[...] = jnp.zeros_like(mark)


def tick(value):
    return pl.pallas_call(
        tick_kernel,
        out_shape=jax.ShapeDtypeStruct((8, LANES), jnp.float32),
        in_specs=[pl.BlockSpec(memory_space=pl.ANY)],
        compiler_params=pltpu.CompilerParams(has_side_effects=True),
    )(value)


def gather_rows(part, axis):
    return lax.all_gather(part, axis, axis=0, tiled=True)


def spread_rows(part):
    count = lax.axis_size("tensor")
    copies = jnp.broadcast_to(part[None], (count,) + part.shape)
    parts = lax.all_to_all(copies, "tensor", split_axis=0, concat_axis=0)
    return parts.reshape((-1,) + part.shape[1:])


def sum_rows(part):
    count = lax.axis_size("tensor")
    blocks = part.reshape((count, part.shape[0] // count) + part.shape[1:])
    parts = lax.all_to_all(blocks, "tensor", split_axis=0, concat_axis=0)
    return jnp.sum(parts.astype(jnp.float32), axis=0)


def scatter_rows(part):
    summed = lax.psum_scatter(
        part.astype(jnp.bfloat16), "tensor", scatter_dimension=0, tiled=True
    )
    return summed.astype(jnp.float32)


def to_owners(grad):
    count = lax.axis_size("dp")
    blocks = grad.astype(jnp.bfloat16).reshape((count, grad.shape[0] // count) + grad.shape[1:])
    return lax.all_to_all(blocks, "dp", split_axis=0, concat_axis=0)


def step(
    tokens,
    cotangent,
    seq_ids,
    block_ids,
    groups,
    qkv_weight,
    out_weight,
    gate_weight,
    down_weight,
    norm_gains,
    qkv_first,
    out_first,
    gate_first,
    down_first,
    gains_first,
    qkv_second,
    out_second,
    gate_second,
    down_second,
    gains_second,
    qkv_outer,
    out_outer,
    gate_outer,
    down_outer,
    gains_outer,
):
    bf16 = jnp.bfloat16
    field_in = tokens.astype(jnp.float32)
    normed_one, scaled_one, factor_one = normed(field_in, norm_gains[0])
    normed_all = spread_rows(normed_one)
    qkv_full = gather_rows(jnp.concatenate([qkv_weight[m].astype(bf16) for m in range(3)], axis=1), "dp")
    out_full = gather_rows(out_weight.T.astype(bf16), "dp")
    gate_full = gather_rows(gate_weight[0].astype(bf16), "dp")
    up_full = gather_rows(gate_weight[1].astype(bf16), "dp")
    down_full = gather_rows(down_weight.T.astype(bf16), "dp")
    cotan_all = spread_rows(after(cotangent, normed_all))

    lo, hi, info = layout_of(seq_ids, block_ids, TILE, TILE)
    cosine, sine_table = rope_tables(lo)
    order = jnp.argsort(groups, stable=True).astype(jnp.int32)

    projected = dot(normed_all, qkv_full)
    mixed_all, queries, keys_all, values_all, logsums = attn_fwd(
        info, projected, cosine, sine_table, lo[:, None], hi[:, None], TILE, TILE
    )
    attn_rows = sum_rows(dot_cols(mixed_all, out_full).astype(bf16))
    residual = field_in + attn_rows
    normed_two, scaled_two, factor_two = normed(residual, norm_gains[1])
    normed_two, gate_full, up_full, down_full = lax.optimization_barrier(
        (normed_two, gate_full, up_full, down_full)
    )
    ffn_input = gather_rows(normed_two, "tensor")
    gate_pre = dot(ffn_input, gate_full)
    up_pre = dot(ffn_input, up_full)
    sigmoid_gate = jax.nn.sigmoid(gate_pre)
    swish = gate_pre * sigmoid_gate
    hidden = (swish * up_pre).astype(bf16)
    down_grad = dot_rows(cotan_all, hidden).astype(bf16)
    down_recv = to_owners(down_grad)
    mark = tick(down_grad)
    hidden, cotan_all = lax.optimization_barrier((hidden, cotan_all, mark))[:2]
    ffn_sum = dot_cols(hidden, down_full).astype(bf16)
    ffn_part = scatter_rows(ffn_sum)
    cotan_all = after(cotan_all, ffn_sum)
    layer_out = (residual + ffn_part).astype(bf16)
    hidden_grad = dot(cotan_all, down_full)
    gate_grad_low = (
        hidden_grad * up_pre * sigmoid_gate * (1.0 + gate_pre * (1.0 - sigmoid_gate))
    ).astype(bf16)
    up_grad_low = (hidden_grad * swish).astype(bf16)
    ffn_back = (dot_cols(gate_grad_low, gate_full) + dot_cols(up_grad_low, up_full)).astype(bf16)
    ffn_back_rows = scatter_rows(ffn_back)
    ffn_kept = after(ffn_input, ffn_back)
    gate_recv = to_owners(dot_rows(ffn_kept, gate_grad_low))
    up_recv = to_owners(dot_rows(ffn_kept, up_grad_low))
    cotan_rows = cotangent.astype(jnp.float32)
    resid_grad = cotan_rows + norm_back(ffn_back_rows, scaled_two, factor_two, norm_gains[1])
    gain_two = jnp.sum(ffn_back_rows * scaled_two, axis=0)
    resid_all = gather_rows(resid_grad.astype(bf16), "tensor")
    mixed_grad = dot(resid_all, out_full).astype(bf16)
    out_recv = to_owners(dot_rows(resid_all, mixed_all))
    raw_grads = attn_bwd(
        info, queries, keys_all, values_all, mixed_all, mixed_grad, logsums,
        cosine, sine_table, lo[None], hi[None], TILE, TILE,
    )
    raw_all = jnp.concatenate(raw_grads, axis=1)
    in_grad_rows = scatter_rows(dot_cols(raw_all, qkv_full))
    qkv_recv = to_owners(dot_rows(normed_all, raw_all))
    tokens_grad = resid_grad + norm_back(in_grad_rows, scaled_one, factor_one, norm_gains[0])
    gain_one = jnp.sum(in_grad_rows * scaled_one, axis=0)
    own_group = (jnp.arange(GROUPS, dtype=jnp.int32) == groups[lax.axis_index("dp")]).astype(
        jnp.float32
    )
    gain_slots = own_group[:, None, None] * jnp.stack([gain_one, gain_two])[None]
    gain_grad = lax.psum(gain_slots, ("dp", "tensor"))
    order = after(order, gain_slots)

    down_new = optimize(
        order, down_recv, down_weight, down_first, down_second, down_outer, 3, turned=True
    )
    gate_half = optimize(
        order, gate_recv, gate_weight, gate_first, gate_second, gate_outer, 2, member=0
    )
    gate_new = optimize(
        order, up_recv, gate_weight, gate_first, gate_second, gate_outer, 2, member=1, before=gate_half
    )
    out_new = optimize(
        order, out_recv, out_weight, out_first, out_second, out_outer, 1, turned=True
    )
    qkv_new = optimize(
        order, after(qkv_recv, gain_grad), qkv_weight, qkv_first, qkv_second, qkv_outer, 0
    )
    gains_new = update(
        norm_gains, gain_grad, gains_first, gains_second, gains_outer, inner_rates[4], decays[4]
    )
    return (layer_out, tokens_grad, *qkv_new, *out_new, *gate_new, *down_new, *gains_new)


def solution(mesh):
    in_specs = (
        P(("dp", "tensor"), None),
        P(("dp", "tensor"), None),
        P("dp"),
        P("dp"),
        P(),
        P(None, "dp", "tensor"),
        P("tensor", "dp"),
        P(None, "dp", "tensor"),
        P("tensor", "dp"),
        P(),
        P(None, None, "dp", "tensor"),
        P(None, "tensor", "dp"),
        P(None, None, "dp", "tensor"),
        P(None, "tensor", "dp"),
        P(),
        P(None, None, "dp", "tensor"),
        P(None, "tensor", "dp"),
        P(None, None, "dp", "tensor"),
        P(None, "tensor", "dp"),
        P(),
        P(None, "dp", "tensor"),
        P("tensor", "dp"),
        P(None, "dp", "tensor"),
        P("tensor", "dp"),
        P(),
    )
    out_specs = (
        P(("dp", "tensor"), None),
        P(("dp", "tensor"), None),
        P(None, None, "dp", "tensor"),
        P(None, None, "dp", "tensor"),
        P(None, "dp", "tensor"),
        P(None, "dp", "tensor"),
        P(None, "dp", "tensor"),
        P(None, "dp", "tensor"),
        P(None, "tensor", "dp"),
        P(None, "tensor", "dp"),
        P("tensor", "dp"),
        P("tensor", "dp"),
        P("tensor", "dp"),
        P("tensor", "dp"),
        P(None, None, "dp", "tensor"),
        P(None, None, "dp", "tensor"),
        P(None, "dp", "tensor"),
        P(None, "dp", "tensor"),
        P(None, "dp", "tensor"),
        P(None, "dp", "tensor"),
        P(None, "tensor", "dp"),
        P(None, "tensor", "dp"),
        P("tensor", "dp"),
        P("tensor", "dp"),
        P("tensor", "dp"),
        P("tensor", "dp"),
        P(),
        P(),
        P(),
        P(),
        P(),
        P(),
    )
    return jax.shard_map(step, mesh=mesh, in_specs=in_specs, out_specs=out_specs, check_vma=False)
```

```python
import functools

import jax
import jax.numpy as jnp
from jax import lax
from jax.experimental import pallas as pl
from jax.experimental.pallas import tpu as pltpu
from jax.sharding import PartitionSpec as P

NT = (((1,), (1,)), ((), ()))
TN = (((0,), (0,)), ((), ()))
NEG = -1e30
LANES = 128


def swap_halves(u):
    lane = lax.broadcasted_iota(jnp.int32, u.shape, 1)
    return jnp.where(lane % 64 < 32, pltpu.roll(u, 96, 1), pltpu.roll(u, 32, 1))


def head_parts(u):
    lane = lax.broadcasted_iota(jnp.int32, u.shape, 1)
    zero = jnp.zeros_like(u)
    return jnp.where(lane < 64, u, zero), jnp.where(lane < 64, zero, u)


def fwd_kernel(tq, tk, info, q_ref, k_ref, v_ref, cos_ref, sin_ref, lo_ref, hi_ref,
               o_ref, qr_ref, kr_ref, vr_ref, lse_ref, q2, v2, m_s, l_s, acc):
    rows = q_ref.shape[0]
    step = 256
    def prep(i, c):
        at = pl.ds(pl.multiple_of(i * step, step), step)
        cos, sin = cos_ref[at, :], sin_ref[at, :]
        q = q_ref[at, :]
        q = (q * cos + swap_halves(q) * sin).astype(jnp.bfloat16) * jnp.bfloat16(0.125)
        k = k_ref[at, :]
        k = (k * cos + swap_halves(k) * sin).astype(jnp.bfloat16)
        v = v_ref[at, :].astype(jnp.bfloat16)
        qr_ref[at, :] = q
        kr_ref[at, :] = k
        vr_ref[at, :] = v
        q2[0, at, :], q2[1, at, :] = head_parts(q)
        v2[0, at, :], v2[1, at, :] = head_parts(v)
        return c
    lax.fori_loop(0, rows // step, prep, 0)

    def q_tile(i, c):
        at = pl.ds(pl.multiple_of(i * tq, tq), tq)
        m_s[...] = jnp.full_like(m_s, -1e29)
        l_s[...] = jnp.zeros_like(l_s)
        acc[...] = jnp.zeros_like(acc)
        first = info[0, i] // tk
        last = (info[3, i] + tk - 1) // tk

        def tile(j, masked):
            ks = pl.multiple_of(j * tk, tk)
            kat = pl.ds(ks, tk)
            k = kr_ref[kat, :]
            if masked:
                key = lax.broadcasted_iota(jnp.int32, (tq, tk), 1) + ks
                ok = (key >= lo_ref[at, :]) & (key < hi_ref[at, :])
            for h in range(2):
                s = lax.dot_general(q2[h, at, :], k, NT, preferred_element_type=jnp.float32)
                if masked:
                    s = jnp.where(ok, s, NEG)
                m_old = m_s[h]
                m_new = jnp.maximum(m_old, jnp.max(s, axis=1, keepdims=True))
                p = jnp.exp(s - m_new[:, :1])
                alpha = jnp.exp(m_old - m_new)
                l_s[h] = alpha * l_s[h] + jnp.sum(p, axis=1, keepdims=True)
                acc[h] = acc[h] * alpha + jnp.dot(
                    p.astype(jnp.bfloat16), v2[h, kat, :], preferred_element_type=jnp.float32)
                m_s[h] = m_new

        def kv_tile(j, c):
            ks = j * tk
            full = (info[1, i] <= ks) & (info[2, i] >= ks + tk)
            @pl.when(full)
            def _():
                tile(j, False)
            @pl.when(jnp.logical_not(full))
            def _():
                tile(j, True)
            return c
        lax.fori_loop(first, last, kv_tile, 0)
        l0, l1 = l_s[0], l_s[1]
        o_ref[at, :] = (acc[0] / l0 + acc[1] / l1).astype(jnp.bfloat16)
        lane = lax.broadcasted_iota(jnp.int32, (tq, LANES), 1)
        lse = jnp.where(lane < 64, m_s[0] + jnp.log(l0), m_s[1] + jnp.log(l1))
        flat = lse.T
        lse_ref[0, 0:1, at] = flat[0:1, :]
        lse_ref[0, 1:2, at] = flat[64:65, :]
        return c
    lax.fori_loop(0, rows // tq, q_tile, 0)


def attn_fwd(info, proj, cos, sin, lo, hi, tq, tk):
    rows, width = proj.shape
    pairs = width // 3 // LANES
    full = lambda p: (0, 0)
    blk = (rows, LANES)
    outs = [jax.ShapeDtypeStruct((rows, pairs * LANES), jnp.bfloat16)] * 4 + [
        jax.ShapeDtypeStruct((pairs, 2, rows), jnp.float32)]
    pair_spec = pl.BlockSpec(blk, lambda p: (0, p))
    area = rows * rows * pairs * 2 * 0.6
    return pl.pallas_call(
        functools.partial(fwd_kernel, tq, tk),
        out_shape=outs,
        grid=(pairs,),
        in_specs=[
            pl.BlockSpec(memory_space=pltpu.SMEM),
            pl.BlockSpec(blk, lambda p: (0, p)),
            pl.BlockSpec(blk, lambda p: (0, p + pairs)),
            pl.BlockSpec(blk, lambda p: (0, p + 2 * pairs)),
            pl.BlockSpec(blk, full), pl.BlockSpec(blk, full),
            pl.BlockSpec((rows, 1), full), pl.BlockSpec((rows, 1), full)],
        out_specs=[pair_spec] * 4 + [pl.BlockSpec((1, 2, rows), lambda p: (p, 0, 0))],
        scratch_shapes=[pltpu.VMEM((2, rows, LANES), jnp.bfloat16), pltpu.VMEM((2, rows, LANES), jnp.bfloat16),
                        pltpu.VMEM((2, tq, LANES), jnp.float32), pltpu.VMEM((2, tq, LANES), jnp.float32),
                        pltpu.VMEM((2, tq, LANES), jnp.float32)],
        compiler_params=pltpu.CompilerParams(vmem_limit_bytes=48 << 20),
        cost_estimate=pl.CostEstimate(flops=int(4 * area * 64), transcendentals=int(area), bytes_accessed=rows * width * 4),
        name="attn_fwd",
    )(info, proj, proj, proj, cos, sin, lo, hi)


def bwd_kernel(tq, tk, info, q_ref, k_ref, v_ref, o_ref, do_ref, lse_ref, cos_ref, sin_ref, lo_ref, hi_ref,
               dq_ref, dk_ref, dv_ref, q2, k2, v2, g2, delta, dq_acc, dk_acc, dv_acc):
    rows = q_ref.shape[0]
    step = 256
    def prep(i, c):
        at = pl.ds(pl.multiple_of(i * step, step), step)
        q2[0, at, :], q2[1, at, :] = head_parts(q_ref[at, :])
        k2[0, at, :], k2[1, at, :] = head_parts(k_ref[at, :])
        v2[0, at, :], v2[1, at, :] = head_parts(v_ref[at, :])
        g = do_ref[at, :]
        g2[0, at, :], g2[1, at, :] = head_parts(g)
        prod = (g.astype(jnp.float32) * o_ref[at, :].astype(jnp.float32)).T
        delta[0:1, at] = jnp.sum(prod[:64], axis=0, keepdims=True)
        delta[1:2, at] = jnp.sum(prod[64:], axis=0, keepdims=True)
        dq_acc[at, :] = jnp.zeros((step, LANES), jnp.float32)
        return c
    lax.fori_loop(0, rows // step, prep, 0)

    def k_tile(j, c):
        ks = pl.multiple_of(j * tk, tk)
        kat = pl.ds(ks, tk)
        dk_acc[...] = jnp.zeros_like(dk_acc)
        dv_acc[...] = jnp.zeros_like(dv_acc)
        first = info[4, j] // tq
        last = (info[5, j] + tq - 1) // tq

        def tile(i, masked):
            at = pl.ds(pl.multiple_of(i * tq, tq), tq)
            if masked:
                key = lax.broadcasted_iota(jnp.int32, (tk, tq), 0) + ks
                ok = (key >= lo_ref[0:1, at]) & (key < hi_ref[0:1, at])
            for h in range(2):
                kh, qh, gh = k2[h, kat, :], q2[h, at, :], g2[h, at, :]
                s = lax.dot_general(kh, qh, NT, preferred_element_type=jnp.float32)
                if masked:
                    s = jnp.where(ok, s, NEG)
                p = jnp.exp(s - lse_ref[0, h:h + 1, at])
                dp = lax.dot_general(v2[h, kat, :], gh, NT, preferred_element_type=jnp.float32)
                ds = (p * (dp - delta[h:h + 1, at])).astype(jnp.bfloat16)
                dv_acc[...] += jnp.dot(p.astype(jnp.bfloat16), gh, preferred_element_type=jnp.float32)
                dk_acc[...] += jnp.dot(ds, qh, preferred_element_type=jnp.float32)
                dq_acc[at, :] += lax.dot_general(ds, kh, TN, preferred_element_type=jnp.float32)

        def q_loop(i, c):
            full = (info[1, i] <= ks) & (info[2, i] >= ks + tk)
            @pl.when(full)
            def _():
                tile(i, False)
            @pl.when(jnp.logical_not(full))
            def _():
                tile(i, True)
            return c
        lax.fori_loop(first, last, q_loop, 0)
        cos, sin = cos_ref[kat, :], sin_ref[kat, :]
        dk = dk_acc[...]
        dk_ref[kat, :] = (dk * cos - swap_halves(dk) * sin).astype(jnp.bfloat16)
        dv_ref[kat, :] = dv_acc[...].astype(jnp.bfloat16)
        return c
    lax.fori_loop(0, rows // tk, k_tile, 0)

    def finish(i, c):
        at = pl.ds(pl.multiple_of(i * step, step), step)
        dq = dq_acc[at, :] * 0.125
        dq_ref[at, :] = (dq * cos_ref[at, :] - swap_halves(dq) * sin_ref[at, :]).astype(jnp.bfloat16)
        return c
    lax.fori_loop(0, rows // step, finish, 0)


def attn_bwd(info, q, k, v, o, do, lse, cos, sin, lo, hi, tq, tk):
    rows, width = q.shape
    pairs = width // LANES
    full = lambda p: (0, 0)
    blk = (rows, LANES)
    pair_spec = pl.BlockSpec(blk, lambda p: (0, p))
    area = rows * rows * pairs * 2 * 0.6
    return pl.pallas_call(
        functools.partial(bwd_kernel, tq, tk),
        out_shape=[jax.ShapeDtypeStruct((rows, width), jnp.bfloat16)] * 3,
        grid=(pairs,),
        in_specs=[pl.BlockSpec(memory_space=pltpu.SMEM)] + [pair_spec] * 5 + [
            pl.BlockSpec((1, 2, rows), lambda p: (p, 0, 0)),
            pl.BlockSpec(blk, full), pl.BlockSpec(blk, full),
            pl.BlockSpec((1, rows), full), pl.BlockSpec((1, rows), full)],
        out_specs=[pair_spec] * 3,
        scratch_shapes=[pltpu.VMEM((2, rows, LANES), jnp.bfloat16)] * 4 + [
            pltpu.VMEM((2, rows), jnp.float32), pltpu.VMEM((rows, LANES), jnp.float32),
            pltpu.VMEM((tk, LANES), jnp.float32), pltpu.VMEM((tk, LANES), jnp.float32)],
        compiler_params=pltpu.CompilerParams(vmem_limit_bytes=48 << 20),
        cost_estimate=pl.CostEstimate(flops=int(10 * area * 64), transcendentals=int(area), bytes_accessed=rows * width * 16),
        name="attn_bwd",
    )(info, q, k, v, o, do, lse, cos, sin, lo, hi)


def layout_of(seq, block, tq, tk):
    rows = seq.shape[0]
    code = seq * 8 + block
    lo = jnp.sum((seq[None, :] < seq[:, None]).astype(jnp.int32), axis=1)
    hi = jnp.sum((code[None, :] <= code[:, None]).astype(jnp.int32), axis=1)
    lt, ht = lo.reshape(-1, tq), hi.reshape(-1, tq)
    start = jnp.arange(rows // tk, dtype=jnp.int32)[:, None] * tk
    qlo = jnp.sum((hi[None, :] <= start).astype(jnp.int32), axis=1)
    qhi = jnp.sum((lo[None, :] < start + tk).astype(jnp.int32), axis=1)
    info = jnp.stack([lt.min(1), lt.max(1), ht.min(1), ht.max(1), qlo, qhi]) if tq == tk else None
    return lo, hi, info


def rope_tables(lo, base=130000.0):
    rows = lo.shape[0]
    where_at = (jnp.arange(rows, dtype=jnp.int32) - lo).astype(jnp.float32)
    inverse = base ** (-(jnp.arange(32, dtype=jnp.float32) * 2.0 / 64))
    ang = where_at[:, None] * inverse[None, :]
    cos, sin = jnp.cos(ang), jnp.sin(ang)
    return jnp.concatenate([cos] * 4, axis=1), jnp.concatenate([-sin, sin, -sin, sin], axis=1)


GROUPS = 4
STEP = 4

norm_eps = 1e-05
beta_first = 0.9
beta_second = 0.95
adam_eps = 1e-08
outer_rate = 0.7
outer_beta = 0.9
inner_rates = (0.04, 0.6, 0.04, 0.02, 0.35)
decays = (0.1, 0.1, 0.1, 0.1, 0.0)
fix_first = 1.0 - beta_first**STEP
fix_second = 1.0 - beta_second**STEP
TILE = 512


def normed(field_rows, gain_row):
    factor = lax.rsqrt(jnp.mean(field_rows * field_rows, axis=-1, keepdims=True) + norm_eps)
    scaled = field_rows * factor
    return ((scaled * gain_row).astype(jnp.bfloat16), scaled, factor)


def norm_back(upstream, scaled, factor, gain_row):
    inside = upstream * gain_row
    return factor * (inside - scaled * jnp.mean(inside * scaled, axis=-1, keepdims=True))


def update(weight, gradient, first_old, second_old, outer_old, step_rate, decay_rate):
    first_new = beta_first * first_old + (1.0 - beta_first) * gradient
    second_new = beta_second * second_old + (1.0 - beta_second) * gradient * gradient
    ratio = first_new / fix_first / (jnp.sqrt(second_new / fix_second) + adam_eps)
    change = step_rate * (jnp.mean(ratio, axis=0) + decay_rate * weight)
    outer_new = outer_beta * outer_old + change
    master = weight - outer_rate * (change + outer_beta * outer_new)
    return [first_new, second_new, change, outer_new, master, master.astype(jnp.bfloat16)]


def opt_kernel(per, turned, parts, rate, decay, order, *refs):
    recvs, (first, second, weight, outer) = refs[:parts], refs[parts : parts + 4]
    first_new, second_new, delta, outer_new, master, low = refs[-6:]
    held = recvs[0].shape[0]
    rows, cols = weight.shape[-2:]
    step_r, step_c = min(rows, 16), min(cols, 256)
    if turned:
        step_r, step_c = min(rows, 128), min(cols, 128)
    lead = (0,) * (len(weight.shape) - 2)

    def chunk(i, carry):
        r = pl.multiple_of((i // (cols // step_c)) * step_r, step_r)
        c = pl.multiple_of((i % (cols // step_c)) * step_c, step_c)
        at = (pl.ds(r, step_r), pl.ds(c, step_c))
        w = weight[lead + at]
        total = jnp.zeros_like(w)
        for g in range(GROUPS):
            grad = None
            for j in range(per):
                source = order[g * per + j]
                block = (pl.ds(c, step_c), pl.ds(r, step_r)) if turned else at
                if parts == 1:
                    part = recvs[0][(source,) + block].astype(jnp.float32)
                else:
                    slot = lax.rem(source, held)
                    own, other = (x[(slot,) + block].astype(jnp.float32) for x in recvs)
                    part = jnp.where(source < held, own, other)
                grad = part if grad is None else grad + part
            if turned:
                grad = grad.T
            m = beta_first * first[(g,) + lead + at] + (1.0 - beta_first) * grad
            v = beta_second * second[(g,) + lead + at] + (1.0 - beta_second) * grad * grad
            first_new[(g,) + lead + at] = m
            second_new[(g,) + lead + at] = v
            total = total + m / (jnp.sqrt(v * (1.0 / fix_second)) + adam_eps)
        change = rate * (total * (1.0 / (fix_first * GROUPS)) + decay * w)
        moved = outer_beta * outer[lead + at] + change
        fresh = w - outer_rate * (change + outer_beta * moved)
        delta[lead + at] = change
        outer_new[lead + at] = moved
        master[lead + at] = fresh
        low[lead + at] = fresh.astype(jnp.bfloat16)
        return carry

    lax.fori_loop(0, (rows // step_r) * (cols // step_c), chunk, 0)


def optimize(order, recv, weight, first, second, outer, position, turned=False, member=None, before=None):
    held = recv[0].shape[0]
    sources = held * len(recv)
    stacked = weight.ndim == 3
    rows, cols = weight.shape[-2:]
    members = weight.shape[0] if stacked and member is None else 1
    base = member or 0
    area = 65536
    if turned:
        br, bc = max(128, min(rows, area // cols)), cols
    else:
        br, bc = max(16, min(rows, area // cols)), cols
    blocks = rows // br
    lead = (1,) if stacked else ()

    def pick(m):
        return (base + m,) if stacked else ()

    if turned:
        recv_spec = pl.BlockSpec((held, bc, br), lambda m, i: (0, 0, i))
    else:
        recv_spec = pl.BlockSpec((held, br, bc), lambda m, i: (0, i, m))
    one = pl.BlockSpec(lead + (br, bc), lambda m, i: pick(m) + (i, 0))
    many = pl.BlockSpec((GROUPS,) + lead + (br, bc), lambda m, i: (0,) + pick(m) + (i, 0))
    f32 = jnp.float32
    outs = [
        jax.ShapeDtypeStruct(first.shape, f32),
        jax.ShapeDtypeStruct(first.shape, f32),
        jax.ShapeDtypeStruct(weight.shape, f32),
        jax.ShapeDtypeStruct(weight.shape, f32),
        jax.ShapeDtypeStruct(weight.shape, f32),
        jax.ShapeDtypeStruct(weight.shape, jnp.bfloat16),
    ]
    operands = [order, *recv, first, second, weight, outer]
    specs = [pl.BlockSpec(memory_space=pltpu.SMEM)] + [recv_spec] * len(recv) + [many, many, one, one]
    aliases = {}
    if before is not None:
        aliases = {len(operands) + k: k for k in range(6)}
        operands += list(before)
        specs += [pl.BlockSpec(memory_space=pl.ANY)] * 6
    count = members * rows * cols
    return pl.pallas_call(
        functools.partial(
            opt_kernel, sources // GROUPS, turned, len(recv), inner_rates[position], decays[position]
        ),
        out_shape=outs,
        grid=(members, blocks),
        in_specs=specs,
        out_specs=[many, many, one, one, one, one],
        input_output_aliases=aliases,
        compiler_params=pltpu.CompilerParams(vmem_limit_bytes=40 << 20),
        cost_estimate=pl.CostEstimate(
            flops=60 * count, transcendentals=8 * count, bytes_accessed=(86 + 2 * sources) * count
        ),
        name="optimize",
    )(*operands)


def dot(left, right):
    return jnp.dot(left, right, preferred_element_type=jnp.float32)


def dot_cols(left, right):
    return lax.dot_general(left, right, (((1,), (1,)), ((), ())), preferred_element_type=jnp.float32)


def dot_rows(left, right):
    return lax.dot_general(left, right, (((0,), (0,)), ((), ())), preferred_element_type=jnp.float32)


def after(value, *others):
    return lax.optimization_barrier((value,) + others)[0]


def tick_kernel(source, mark):
    mark[...] = jnp.zeros_like(mark)


def tick(value):
    return pl.pallas_call(
        tick_kernel,
        out_shape=jax.ShapeDtypeStruct((8, LANES), jnp.float32),
        in_specs=[pl.BlockSpec(memory_space=pl.ANY)],
        compiler_params=pltpu.CompilerParams(has_side_effects=True),
    )(value)


def gather_rows(part, axis):
    return lax.all_gather(part, axis, axis=0, tiled=True)


def spread_rows(part):
    count = lax.axis_size("tensor")
    copies = jnp.broadcast_to(part[None], (count,) + part.shape)
    parts = lax.all_to_all(copies, "tensor", split_axis=0, concat_axis=0)
    return parts.reshape((-1,) + part.shape[1:])


def sum_rows(part):
    count = lax.axis_size("tensor")
    blocks = part.reshape((count, part.shape[0] // count) + part.shape[1:])
    parts = lax.all_to_all(blocks, "tensor", split_axis=0, concat_axis=0)
    return jnp.sum(parts.astype(jnp.float32), axis=0)


def scatter_rows(part):
    summed = lax.psum_scatter(
        part.astype(jnp.bfloat16), "tensor", scatter_dimension=0, tiled=True
    )
    return summed.astype(jnp.float32)


def to_half(grad):
    count = lax.axis_size("dp")
    near = count // 2
    blocks = grad.astype(jnp.bfloat16).reshape((near, grad.shape[0] // near) + grad.shape[1:])
    halves = [list(range(near)), list(range(near, count))]
    return lax.all_to_all(blocks, "dp", split_axis=0, concat_axis=0, axis_index_groups=halves)


def to_partner(part):
    count = lax.axis_size("dp")
    return lax.ppermute(part, "dp", [(i, (i + count // 2) % count) for i in range(count)])


def half_cols(rows):
    near = lax.axis_size("dp") // 2
    wide = rows.shape[1] // 2
    return lax.dynamic_slice_in_dim(rows, lax.axis_index("dp") // near * wide, wide, axis=1)


def to_owners(grad):
    count = lax.axis_size("dp")
    blocks = grad.astype(jnp.bfloat16).reshape((count, grad.shape[0] // count) + grad.shape[1:])
    return lax.all_to_all(blocks, "dp", split_axis=0, concat_axis=0)


def step(
    tokens,
    cotangent,
    seq_ids,
    block_ids,
    groups,
    qkv_weight,
    out_weight,
    gate_weight,
    down_weight,
    norm_gains,
    qkv_first,
    out_first,
    gate_first,
    down_first,
    gains_first,
    qkv_second,
    out_second,
    gate_second,
    down_second,
    gains_second,
    qkv_outer,
    out_outer,
    gate_outer,
    down_outer,
    gains_outer,
):
    bf16 = jnp.bfloat16
    field_in = tokens.astype(jnp.float32)
    normed_one, scaled_one, factor_one = normed(field_in, norm_gains[0])
    normed_all = spread_rows(normed_one)
    qkv_full = gather_rows(jnp.concatenate([qkv_weight[m].astype(bf16) for m in range(3)], axis=1), "dp")
    out_full = gather_rows(out_weight.T.astype(bf16), "dp")
    gate_full = gather_rows(gate_weight[0].astype(bf16), "dp")
    up_full = gather_rows(gate_weight[1].astype(bf16), "dp")
    down_full = gather_rows(down_weight.T.astype(bf16), "dp")
    cotan_all = spread_rows(after(cotangent, normed_all))

    other_cotan = to_partner(cotangent)
    lo, hi, info = layout_of(seq_ids, block_ids, TILE, TILE)
    cosine, sine_table = rope_tables(lo)
    order = jnp.argsort(groups, stable=True).astype(jnp.int32)

    projected = dot(normed_all, qkv_full)
    mixed_all, queries, keys_all, values_all, logsums = attn_fwd(
        info, projected, cosine, sine_table, lo[:, None], hi[:, None], TILE, TILE
    )
    attn_rows = sum_rows(dot_cols(mixed_all, out_full).astype(bf16))
    residual = field_in + attn_rows
    normed_two, scaled_two, factor_two = normed(residual, norm_gains[1])
    other_two = to_partner(normed_two)
    normed_two, gate_full, up_full = lax.optimization_barrier((normed_two, gate_full, up_full, tick(normed_two)))[:3]
    ffn_input = spread_rows(normed_two)
    other_dy = gather_rows(after(other_cotan, ffn_input), "tensor")
    other_input = gather_rows(other_two, "tensor")

    gate_pre = dot(ffn_input, gate_full)
    up_pre = dot(ffn_input, up_full)
    sigmoid_gate = jax.nn.sigmoid(gate_pre)
    swish = gate_pre * sigmoid_gate
    hidden = (swish * up_pre).astype(bf16)
    down_grad = dot_rows(half_cols(cotan_all), hidden).astype(bf16)
    down_recv = to_half(down_grad)
    cotan_all = after(cotan_all, tick(down_grad))
    hidden_grad = dot(cotan_all, down_full)
    gate_grad_low = (
        hidden_grad * up_pre * sigmoid_gate * (1.0 + gate_pre * (1.0 - sigmoid_gate))
    ).astype(bf16)
    up_grad_low = (hidden_grad * swish).astype(bf16)
    ffn_back = (dot_cols(gate_grad_low, gate_full) + dot_cols(up_grad_low, up_full)).astype(bf16)
    ffn_back_rows = scatter_rows(ffn_back)
    input_half = half_cols(after(ffn_input, ffn_back))
    gate_grad = dot_rows(input_half, gate_grad_low).astype(bf16)
    gate_recv = to_half(gate_grad)
    up_grad = dot_rows(input_half, up_grad_low).astype(bf16)
    up_recv = to_half(up_grad)
    hidden = after(hidden, gate_grad, up_grad)
    ffn_sum = dot_cols(hidden, down_full).astype(bf16)
    ffn_part = scatter_rows(ffn_sum)
    layer_out = (residual + ffn_part).astype(bf16)

    other_input = after(other_input, ffn_sum)
    gate_pre = dot(other_input, gate_full)
    up_pre = dot(other_input, up_full)
    sigmoid_gate = jax.nn.sigmoid(gate_pre)
    swish = gate_pre * sigmoid_gate
    hidden = (swish * up_pre).astype(bf16)
    mark = tick(hidden)
    other_dy = after(other_dy, mark)
    down_grad = dot_rows(half_cols(other_dy), hidden).astype(bf16)
    down_recv2 = to_half(down_grad)
    hidden_grad = dot(after(other_dy, down_grad), down_full)
    gate_grad_low = (
        hidden_grad * up_pre * sigmoid_gate * (1.0 + gate_pre * (1.0 - sigmoid_gate))
    ).astype(bf16)
    up_grad_low = (hidden_grad * swish).astype(bf16)
    input_half = half_cols(other_input)
    gate_grad = dot_rows(input_half, gate_grad_low).astype(bf16)
    gate_recv2 = to_half(gate_grad)
    up_grad = dot_rows(input_half, up_grad_low).astype(bf16)
    up_recv2 = to_half(up_grad)
    mark = tick(up_grad)

    cotan_rows = cotangent.astype(jnp.float32)
    resid_grad = cotan_rows + norm_back(ffn_back_rows, scaled_two, factor_two, norm_gains[1])
    gain_two = jnp.sum(ffn_back_rows * scaled_two, axis=0)
    resid_all = gather_rows(resid_grad.astype(bf16), "tensor")
    resid_all = after(resid_all, mark)
    mixed_grad = dot(resid_all, out_full).astype(bf16)
    out_recv = to_owners(dot_rows(resid_all, mixed_all))
    raw_grads = attn_bwd(
        info, queries, keys_all, values_all, mixed_all, mixed_grad, logsums,
        cosine, sine_table, lo[None], hi[None], TILE, TILE,
    )
    raw_all = jnp.concatenate(raw_grads, axis=1)
    in_grad_rows = scatter_rows(dot_cols(raw_all, qkv_full))
    qkv_recv = to_owners(dot_rows(normed_all, raw_all))
    tokens_grad = resid_grad + norm_back(in_grad_rows, scaled_one, factor_one, norm_gains[0])
    gain_one = jnp.sum(in_grad_rows * scaled_one, axis=0)
    own_group = (jnp.arange(GROUPS, dtype=jnp.int32) == groups[lax.axis_index("dp")]).astype(
        jnp.float32
    )
    gain_slots = own_group[:, None, None] * jnp.stack([gain_one, gain_two])[None]
    gain_grad = lax.psum(gain_slots, ("dp", "tensor"))
    order = after(order, gain_slots)
    near = lax.axis_size("dp") // 2
    side = order // near != lax.axis_index("dp") // near
    near_order = order % near + near * side.astype(jnp.int32)

    down_new = optimize(
        near_order, (down_recv, down_recv2), down_weight, down_first, down_second, down_outer, 3, turned=True
    )
    gate_half = optimize(
        near_order, (gate_recv, gate_recv2), gate_weight, gate_first, gate_second, gate_outer, 2, member=0
    )
    gate_new = optimize(
        near_order, (up_recv, up_recv2), gate_weight, gate_first, gate_second, gate_outer, 2, member=1, before=gate_half
    )
    out_new = optimize(
        order, (out_recv,), out_weight, out_first, out_second, out_outer, 1, turned=True
    )
    qkv_new = optimize(
        order, (after(qkv_recv, gain_grad),), qkv_weight, qkv_first, qkv_second, qkv_outer, 0
    )
    gains_new = update(
        norm_gains, gain_grad, gains_first, gains_second, gains_outer, inner_rates[4], decays[4]
    )
    return (layer_out, tokens_grad, *qkv_new, *out_new, *gate_new, *down_new, *gains_new)


def solution(mesh):
    in_specs = (
        P(("dp", "tensor"), None),
        P(("dp", "tensor"), None),
        P("dp"),
        P("dp"),
        P(),
        P(None, "dp", "tensor"),
        P("tensor", "dp"),
        P(None, "dp", "tensor"),
        P("tensor", "dp"),
        P(),
        P(None, None, "dp", "tensor"),
        P(None, "tensor", "dp"),
        P(None, None, "dp", "tensor"),
        P(None, "tensor", "dp"),
        P(),
        P(None, None, "dp", "tensor"),
        P(None, "tensor", "dp"),
        P(None, None, "dp", "tensor"),
        P(None, "tensor", "dp"),
        P(),
        P(None, "dp", "tensor"),
        P("tensor", "dp"),
        P(None, "dp", "tensor"),
        P("tensor", "dp"),
        P(),
    )
    out_specs = (
        P(("dp", "tensor"), None),
        P(("dp", "tensor"), None),
        P(None, None, "dp", "tensor"),
        P(None, None, "dp", "tensor"),
        P(None, "dp", "tensor"),
        P(None, "dp", "tensor"),
        P(None, "dp", "tensor"),
        P(None, "dp", "tensor"),
        P(None, "tensor", "dp"),
        P(None, "tensor", "dp"),
        P("tensor", "dp"),
        P("tensor", "dp"),
        P("tensor", "dp"),
        P("tensor", "dp"),
        P(None, None, "dp", "tensor"),
        P(None, None, "dp", "tensor"),
        P(None, "dp", "tensor"),
        P(None, "dp", "tensor"),
        P(None, "dp", "tensor"),
        P(None, "dp", "tensor"),
        P(None, "tensor", "dp"),
        P(None, "tensor", "dp"),
        P("tensor", "dp"),
        P("tensor", "dp"),
        P("tensor", "dp"),
        P("tensor", "dp"),
        P(),
        P(),
        P(),
        P(),
        P(),
        P(),
    )
    return jax.shard_map(step, mesh=mesh, in_specs=in_specs, out_specs=out_specs, check_vma=False)
```

```python
import functools

import jax
import jax.numpy as jnp
from jax import lax
from jax.experimental import pallas as pl
from jax.experimental.pallas import tpu as pltpu
from jax.sharding import PartitionSpec as P

NT = (((1,), (1,)), ((), ()))
TN = (((0,), (0,)), ((), ()))
NEG = -1e30
LANES = 128


def swap_halves(u):
    lane = lax.broadcasted_iota(jnp.int32, u.shape, 1)
    return jnp.where(lane % 64 < 32, pltpu.roll(u, 96, 1), pltpu.roll(u, 32, 1))


def head_parts(u):
    lane = lax.broadcasted_iota(jnp.int32, u.shape, 1)
    zero = jnp.zeros_like(u)
    return jnp.where(lane < 64, u, zero), jnp.where(lane < 64, zero, u)


def fwd_kernel(tq, tk, info, q_ref, k_ref, v_ref, cos_ref, sin_ref, lo_ref, hi_ref,
               o_ref, qr_ref, kr_ref, vr_ref, lse_ref, q2, v2, m_s, l_s, acc):
    rows = q_ref.shape[0]
    step = 256
    def prep(i, c):
        at = pl.ds(pl.multiple_of(i * step, step), step)
        cos, sin = cos_ref[at, :], sin_ref[at, :]
        q = q_ref[at, :]
        q = (q * cos + swap_halves(q) * sin).astype(jnp.bfloat16) * jnp.bfloat16(0.125)
        k = k_ref[at, :]
        k = (k * cos + swap_halves(k) * sin).astype(jnp.bfloat16)
        v = v_ref[at, :].astype(jnp.bfloat16)
        qr_ref[at, :] = q
        kr_ref[at, :] = k
        vr_ref[at, :] = v
        q2[0, at, :], q2[1, at, :] = head_parts(q)
        v2[0, at, :], v2[1, at, :] = head_parts(v)
        return c
    lax.fori_loop(0, rows // step, prep, 0)

    def q_tile(i, c):
        at = pl.ds(pl.multiple_of(i * tq, tq), tq)
        m_s[...] = jnp.full_like(m_s, -1e29)
        l_s[...] = jnp.zeros_like(l_s)
        acc[...] = jnp.zeros_like(acc)
        first = info[0, i] // tk
        last = (info[3, i] + tk - 1) // tk

        def tile(j, masked):
            ks = pl.multiple_of(j * tk, tk)
            kat = pl.ds(ks, tk)
            k = kr_ref[kat, :]
            if masked:
                key = lax.broadcasted_iota(jnp.int32, (tq, tk), 1) + ks
                ok = (key >= lo_ref[at, :]) & (key < hi_ref[at, :])
            for h in range(2):
                s = lax.dot_general(q2[h, at, :], k, NT, preferred_element_type=jnp.float32)
                if masked:
                    s = jnp.where(ok, s, NEG)
                m_old = m_s[h]
                m_new = jnp.maximum(m_old, jnp.max(s, axis=1, keepdims=True))
                p = jnp.exp(s - m_new[:, :1])
                alpha = jnp.exp(m_old - m_new)
                l_s[h] = alpha * l_s[h] + jnp.sum(p, axis=1, keepdims=True)
                acc[h] = acc[h] * alpha + jnp.dot(
                    p.astype(jnp.bfloat16), v2[h, kat, :], preferred_element_type=jnp.float32)
                m_s[h] = m_new

        def kv_tile(j, c):
            ks = j * tk
            full = (info[1, i] <= ks) & (info[2, i] >= ks + tk)
            @pl.when(full)
            def _():
                tile(j, False)
            @pl.when(jnp.logical_not(full))
            def _():
                tile(j, True)
            return c
        lax.fori_loop(first, last, kv_tile, 0)
        l0, l1 = l_s[0], l_s[1]
        o_ref[at, :] = (acc[0] / l0 + acc[1] / l1).astype(jnp.bfloat16)
        lane = lax.broadcasted_iota(jnp.int32, (tq, LANES), 1)
        lse = jnp.where(lane < 64, m_s[0] + jnp.log(l0), m_s[1] + jnp.log(l1))
        flat = lse.T
        lse_ref[0, 0:1, at] = flat[0:1, :]
        lse_ref[0, 1:2, at] = flat[64:65, :]
        return c
    lax.fori_loop(0, rows // tq, q_tile, 0)


def attn_fwd(info, proj, cos, sin, lo, hi, tq, tk):
    rows, width = proj.shape
    pairs = width // 3 // LANES
    full = lambda p: (0, 0)
    blk = (rows, LANES)
    outs = [jax.ShapeDtypeStruct((rows, pairs * LANES), jnp.bfloat16)] * 4 + [
        jax.ShapeDtypeStruct((pairs, 2, rows), jnp.float32)]
    pair_spec = pl.BlockSpec(blk, lambda p: (0, p))
    area = rows * rows * pairs * 2 * 0.6
    return pl.pallas_call(
        functools.partial(fwd_kernel, tq, tk),
        out_shape=outs,
        grid=(pairs,),
        in_specs=[
            pl.BlockSpec(memory_space=pltpu.SMEM),
            pl.BlockSpec(blk, lambda p: (0, p)),
            pl.BlockSpec(blk, lambda p: (0, p + pairs)),
            pl.BlockSpec(blk, lambda p: (0, p + 2 * pairs)),
            pl.BlockSpec(blk, full), pl.BlockSpec(blk, full),
            pl.BlockSpec((rows, 1), full), pl.BlockSpec((rows, 1), full)],
        out_specs=[pair_spec] * 4 + [pl.BlockSpec((1, 2, rows), lambda p: (p, 0, 0))],
        scratch_shapes=[pltpu.VMEM((2, rows, LANES), jnp.bfloat16), pltpu.VMEM((2, rows, LANES), jnp.bfloat16),
                        pltpu.VMEM((2, tq, LANES), jnp.float32), pltpu.VMEM((2, tq, LANES), jnp.float32),
                        pltpu.VMEM((2, tq, LANES), jnp.float32)],
        compiler_params=pltpu.CompilerParams(vmem_limit_bytes=48 << 20),
        cost_estimate=pl.CostEstimate(flops=int(4 * area * 64), transcendentals=int(area), bytes_accessed=rows * width * 4),
        name="attn_fwd",
    )(info, proj, proj, proj, cos, sin, lo, hi)


def bwd_kernel(tq, tk, info, q_ref, k_ref, v_ref, o_ref, do_ref, lse_ref, cos_ref, sin_ref, lo_ref, hi_ref,
               dq_ref, dk_ref, dv_ref, q2, k2, v2, g2, delta, dq_acc, dk_acc, dv_acc):
    rows = q_ref.shape[0]
    step = 256
    def prep(i, c):
        at = pl.ds(pl.multiple_of(i * step, step), step)
        q2[0, at, :], q2[1, at, :] = head_parts(q_ref[at, :])
        k2[0, at, :], k2[1, at, :] = head_parts(k_ref[at, :])
        v2[0, at, :], v2[1, at, :] = head_parts(v_ref[at, :])
        g = do_ref[at, :]
        g2[0, at, :], g2[1, at, :] = head_parts(g)
        prod = (g.astype(jnp.float32) * o_ref[at, :].astype(jnp.float32)).T
        delta[0:1, at] = jnp.sum(prod[:64], axis=0, keepdims=True)
        delta[1:2, at] = jnp.sum(prod[64:], axis=0, keepdims=True)
        dq_acc[at, :] = jnp.zeros((step, LANES), jnp.float32)
        return c
    lax.fori_loop(0, rows // step, prep, 0)

    def k_tile(j, c):
        ks = pl.multiple_of(j * tk, tk)
        kat = pl.ds(ks, tk)
        dk_acc[...] = jnp.zeros_like(dk_acc)
        dv_acc[...] = jnp.zeros_like(dv_acc)
        first = info[4, j] // tq
        last = (info[5, j] + tq - 1) // tq

        def tile(i, masked):
            at = pl.ds(pl.multiple_of(i * tq, tq), tq)
            if masked:
                key = lax.broadcasted_iota(jnp.int32, (tk, tq), 0) + ks
                ok = (key >= lo_ref[0:1, at]) & (key < hi_ref[0:1, at])
            for h in range(2):
                kh, qh, gh = k2[h, kat, :], q2[h, at, :], g2[h, at, :]
                s = lax.dot_general(kh, qh, NT, preferred_element_type=jnp.float32)
                if masked:
                    s = jnp.where(ok, s, NEG)
                p = jnp.exp(s - lse_ref[0, h:h + 1, at])
                dp = lax.dot_general(v2[h, kat, :], gh, NT, preferred_element_type=jnp.float32)
                ds = (p * (dp - delta[h:h + 1, at])).astype(jnp.bfloat16)
                dv_acc[...] += jnp.dot(p.astype(jnp.bfloat16), gh, preferred_element_type=jnp.float32)
                dk_acc[...] += jnp.dot(ds, qh, preferred_element_type=jnp.float32)
                dq_acc[at, :] += lax.dot_general(ds, kh, TN, preferred_element_type=jnp.float32)

        def q_loop(i, c):
            full = (info[1, i] <= ks) & (info[2, i] >= ks + tk)
            @pl.when(full)
            def _():
                tile(i, False)
            @pl.when(jnp.logical_not(full))
            def _():
                tile(i, True)
            return c
        lax.fori_loop(first, last, q_loop, 0)
        cos, sin = cos_ref[kat, :], sin_ref[kat, :]
        dk = dk_acc[...]
        dk_ref[kat, :] = (dk * cos - swap_halves(dk) * sin).astype(jnp.bfloat16)
        dv_ref[kat, :] = dv_acc[...].astype(jnp.bfloat16)
        return c
    lax.fori_loop(0, rows // tk, k_tile, 0)

    def finish(i, c):
        at = pl.ds(pl.multiple_of(i * step, step), step)
        dq = dq_acc[at, :] * 0.125
        dq_ref[at, :] = (dq * cos_ref[at, :] - swap_halves(dq) * sin_ref[at, :]).astype(jnp.bfloat16)
        return c
    lax.fori_loop(0, rows // step, finish, 0)


def attn_bwd(info, q, k, v, o, do, lse, cos, sin, lo, hi, tq, tk):
    rows, width = q.shape
    pairs = width // LANES
    full = lambda p: (0, 0)
    blk = (rows, LANES)
    pair_spec = pl.BlockSpec(blk, lambda p: (0, p))
    area = rows * rows * pairs * 2 * 0.6
    return pl.pallas_call(
        functools.partial(bwd_kernel, tq, tk),
        out_shape=[jax.ShapeDtypeStruct((rows, width), jnp.bfloat16)] * 3,
        grid=(pairs,),
        in_specs=[pl.BlockSpec(memory_space=pltpu.SMEM)] + [pair_spec] * 5 + [
            pl.BlockSpec((1, 2, rows), lambda p: (p, 0, 0)),
            pl.BlockSpec(blk, full), pl.BlockSpec(blk, full),
            pl.BlockSpec((1, rows), full), pl.BlockSpec((1, rows), full)],
        out_specs=[pair_spec] * 3,
        scratch_shapes=[pltpu.VMEM((2, rows, LANES), jnp.bfloat16)] * 4 + [
            pltpu.VMEM((2, rows), jnp.float32), pltpu.VMEM((rows, LANES), jnp.float32),
            pltpu.VMEM((tk, LANES), jnp.float32), pltpu.VMEM((tk, LANES), jnp.float32)],
        compiler_params=pltpu.CompilerParams(vmem_limit_bytes=48 << 20),
        cost_estimate=pl.CostEstimate(flops=int(10 * area * 64), transcendentals=int(area), bytes_accessed=rows * width * 16),
        name="attn_bwd",
    )(info, q, k, v, o, do, lse, cos, sin, lo, hi)


def layout_of(seq, block, tq, tk):
    rows = seq.shape[0]
    code = seq * 8 + block
    lo = jnp.sum((seq[None, :] < seq[:, None]).astype(jnp.int32), axis=1)
    hi = jnp.sum((code[None, :] <= code[:, None]).astype(jnp.int32), axis=1)
    lt, ht = lo.reshape(-1, tq), hi.reshape(-1, tq)
    start = jnp.arange(rows // tk, dtype=jnp.int32)[:, None] * tk
    qlo = jnp.sum((hi[None, :] <= start).astype(jnp.int32), axis=1)
    qhi = jnp.sum((lo[None, :] < start + tk).astype(jnp.int32), axis=1)
    info = jnp.stack([lt.min(1), lt.max(1), ht.min(1), ht.max(1), qlo, qhi]) if tq == tk else None
    return lo, hi, info


def rope_tables(lo, base=130000.0):
    rows = lo.shape[0]
    where_at = (jnp.arange(rows, dtype=jnp.int32) - lo).astype(jnp.float32)
    inverse = base ** (-(jnp.arange(32, dtype=jnp.float32) * 2.0 / 64))
    ang = where_at[:, None] * inverse[None, :]
    cos, sin = jnp.cos(ang), jnp.sin(ang)
    return jnp.concatenate([cos] * 4, axis=1), jnp.concatenate([-sin, sin, -sin, sin], axis=1)


GROUPS = 4
STEP = 4

norm_eps = 1e-05
beta_first = 0.9
beta_second = 0.95
adam_eps = 1e-08
outer_rate = 0.7
outer_beta = 0.9
inner_rates = (0.04, 0.6, 0.04, 0.02, 0.35)
decays = (0.1, 0.1, 0.1, 0.1, 0.0)
fix_first = 1.0 - beta_first**STEP
fix_second = 1.0 - beta_second**STEP
TILE = 512


def normed(field_rows, gain_row):
    factor = lax.rsqrt(jnp.mean(field_rows * field_rows, axis=-1, keepdims=True) + norm_eps)
    scaled = field_rows * factor
    return ((scaled * gain_row).astype(jnp.bfloat16), scaled, factor)


def norm_back(upstream, scaled, factor, gain_row):
    inside = upstream * gain_row
    return factor * (inside - scaled * jnp.mean(inside * scaled, axis=-1, keepdims=True))


def update(weight, gradient, first_old, second_old, outer_old, step_rate, decay_rate):
    first_new = beta_first * first_old + (1.0 - beta_first) * gradient
    second_new = beta_second * second_old + (1.0 - beta_second) * gradient * gradient
    ratio = first_new / fix_first / (jnp.sqrt(second_new / fix_second) + adam_eps)
    change = step_rate * (jnp.mean(ratio, axis=0) + decay_rate * weight)
    outer_new = outer_beta * outer_old + change
    master = weight - outer_rate * (change + outer_beta * outer_new)
    return [first_new, second_new, change, outer_new, master, master.astype(jnp.bfloat16)]


def opt_kernel(per, turned, parts, rate, decay, order, *refs):
    recvs, (first, second, weight, outer) = refs[:parts], refs[parts : parts + 4]
    first_new, second_new, delta, outer_new, master, low = refs[-6:]
    held = recvs[0].shape[0]
    rows, cols = weight.shape[-2:]
    step_r, step_c = min(rows, 16), min(cols, 256)
    if turned:
        step_r, step_c = min(rows, 128), min(cols, 128)
    lead = (0,) * (len(weight.shape) - 2)

    def chunk(i, carry):
        r = pl.multiple_of((i // (cols // step_c)) * step_r, step_r)
        c = pl.multiple_of((i % (cols // step_c)) * step_c, step_c)
        at = (pl.ds(r, step_r), pl.ds(c, step_c))
        w = weight[lead + at]
        total = jnp.zeros_like(w)
        for g in range(GROUPS):
            grad = None
            for j in range(per):
                source = order[g * per + j]
                block = (pl.ds(c, step_c), pl.ds(r, step_r)) if turned else at
                if parts == 1:
                    part = recvs[0][(source,) + block].astype(jnp.float32)
                else:
                    slot = lax.rem(source, held)
                    own, other = (x[(slot,) + block].astype(jnp.float32) for x in recvs)
                    part = jnp.where(source < held, own, other)
                grad = part if grad is None else grad + part
            if turned:
                grad = grad.T
            m = beta_first * first[(g,) + lead + at] + (1.0 - beta_first) * grad
            v = beta_second * second[(g,) + lead + at] + (1.0 - beta_second) * grad * grad
            first_new[(g,) + lead + at] = m
            second_new[(g,) + lead + at] = v
            total = total + m / (jnp.sqrt(v * (1.0 / fix_second)) + adam_eps)
        change = rate * (total * (1.0 / (fix_first * GROUPS)) + decay * w)
        moved = outer_beta * outer[lead + at] + change
        fresh = w - outer_rate * (change + outer_beta * moved)
        delta[lead + at] = change
        outer_new[lead + at] = moved
        master[lead + at] = fresh
        low[lead + at] = fresh.astype(jnp.bfloat16)
        return carry

    lax.fori_loop(0, (rows // step_r) * (cols // step_c), chunk, 0)


def optimize(order, recv, weight, first, second, outer, position, turned=False, member=None, before=None):
    held = recv[0].shape[0]
    sources = held * len(recv)
    stacked = weight.ndim == 3
    rows, cols = weight.shape[-2:]
    members = weight.shape[0] if stacked and member is None else 1
    base = member or 0
    area = 65536
    if turned:
        br, bc = max(128, min(rows, area // cols)), cols
    else:
        br, bc = max(16, min(rows, area // cols)), cols
    blocks = rows // br
    lead = (1,) if stacked else ()

    def pick(m):
        return (base + m,) if stacked else ()

    if turned:
        recv_spec = pl.BlockSpec((held, bc, br), lambda m, i: (0, 0, i))
    else:
        recv_spec = pl.BlockSpec((held, br, bc), lambda m, i: (0, i, m))
    recv_specs = [recv_spec]
    if len(recv) > 1:
        place = 2 if turned else base
        if turned:
            recv_specs.append(pl.BlockSpec((held, bc, br), lambda m, i: (0, place, i)))
        else:
            recv_specs.append(pl.BlockSpec((held, br, bc), lambda m, i: (0, place * blocks + i, 0)))
    one = pl.BlockSpec(lead + (br, bc), lambda m, i: pick(m) + (i, 0))
    many = pl.BlockSpec((GROUPS,) + lead + (br, bc), lambda m, i: (0,) + pick(m) + (i, 0))
    f32 = jnp.float32
    outs = [
        jax.ShapeDtypeStruct(first.shape, f32),
        jax.ShapeDtypeStruct(first.shape, f32),
        jax.ShapeDtypeStruct(weight.shape, f32),
        jax.ShapeDtypeStruct(weight.shape, f32),
        jax.ShapeDtypeStruct(weight.shape, f32),
        jax.ShapeDtypeStruct(weight.shape, jnp.bfloat16),
    ]
    operands = [order, *recv, first, second, weight, outer]
    specs = [pl.BlockSpec(memory_space=pltpu.SMEM)] + recv_specs + [many, many, one, one]
    aliases = {}
    if before is not None:
        aliases = {len(operands) + k: k for k in range(6)}
        operands += list(before)
        specs += [pl.BlockSpec(memory_space=pl.ANY)] * 6
    count = members * rows * cols
    return pl.pallas_call(
        functools.partial(
            opt_kernel, sources // GROUPS, turned, len(recv), inner_rates[position], decays[position]
        ),
        out_shape=outs,
        grid=(members, blocks),
        in_specs=specs,
        out_specs=[many, many, one, one, one, one],
        input_output_aliases=aliases,
        compiler_params=pltpu.CompilerParams(vmem_limit_bytes=40 << 20),
        cost_estimate=pl.CostEstimate(
            flops=60 * count, transcendentals=8 * count, bytes_accessed=(86 + 2 * sources) * count
        ),
        name="optimize",
    )(*operands)


def dot(left, right):
    return jnp.dot(left, right, preferred_element_type=jnp.float32)


def dot_cols(left, right):
    return lax.dot_general(left, right, (((1,), (1,)), ((), ())), preferred_element_type=jnp.float32)


def dot_rows(left, right):
    return lax.dot_general(left, right, (((0,), (0,)), ((), ())), preferred_element_type=jnp.float32)


def after(value, *others):
    return lax.optimization_barrier((value,) + others)[0]


def tick_kernel(*refs):
    refs[-1][...] = jnp.zeros_like(refs[-1])


def tick(*values):
    return pl.pallas_call(
        tick_kernel,
        out_shape=jax.ShapeDtypeStruct((8, LANES), jnp.float32),
        in_specs=[pl.BlockSpec(memory_space=pl.ANY)] * len(values),
        compiler_params=pltpu.CompilerParams(has_side_effects=True),
    )(*values)


def gather_rows(part, axis):
    return lax.all_gather(part, axis, axis=0, tiled=True)


def copies_of(part):
    return jnp.broadcast_to(part[None], (lax.axis_size("tensor"),) + part.shape)


def spread_rows(copies):
    parts = lax.all_to_all(copies, "tensor", split_axis=0, concat_axis=0)
    return parts.reshape((-1,) + copies.shape[2:])


def sum_rows(part):
    count = lax.axis_size("tensor")
    blocks = part.reshape((count, part.shape[0] // count) + part.shape[1:])
    parts = lax.all_to_all(blocks, "tensor", split_axis=0, concat_axis=0)
    return jnp.sum(parts.astype(jnp.float32), axis=0)


def scatter_rows(part):
    summed = lax.psum_scatter(
        part.astype(jnp.bfloat16), "tensor", scatter_dimension=0, tiled=True
    )
    return summed.astype(jnp.float32)


def to_half(grad):
    count = lax.axis_size("dp")
    near = count // 2
    blocks = grad.astype(jnp.bfloat16).reshape((near, grad.shape[0] // near) + grad.shape[1:])
    halves = [list(range(near)), list(range(near, count))]
    return lax.all_to_all(blocks, "dp", split_axis=0, concat_axis=0, axis_index_groups=halves)


def to_partner(part):
    count = lax.axis_size("dp")
    return lax.ppermute(part, "dp", [(i, (i + count // 2) % count) for i in range(count)])


def half_cols(rows):
    near = lax.axis_size("dp") // 2
    wide = rows.shape[1] // 2
    return lax.dynamic_slice_in_dim(rows, lax.axis_index("dp") // near * wide, wide, axis=1)


def to_owners(grad):
    count = lax.axis_size("dp")
    blocks = grad.astype(jnp.bfloat16).reshape((count, grad.shape[0] // count) + grad.shape[1:])
    return lax.all_to_all(blocks, "dp", split_axis=0, concat_axis=0)


def step(
    tokens,
    cotangent,
    seq_ids,
    block_ids,
    groups,
    qkv_weight,
    out_weight,
    gate_weight,
    down_weight,
    norm_gains,
    qkv_first,
    out_first,
    gate_first,
    down_first,
    gains_first,
    qkv_second,
    out_second,
    gate_second,
    down_second,
    gains_second,
    qkv_outer,
    out_outer,
    gate_outer,
    down_outer,
    gains_outer,
):
    bf16 = jnp.bfloat16
    field_in = tokens.astype(jnp.float32)
    normed_one, scaled_one, factor_one = normed(field_in, norm_gains[0])
    normed_all = spread_rows(copies_of(normed_one))
    qkv_full = gather_rows(jnp.concatenate([qkv_weight[m].astype(bf16) for m in range(3)], axis=1), "dp")
    out_full = gather_rows(out_weight.T.astype(bf16), "dp")
    gate_full = gather_rows(gate_weight[0].astype(bf16), "dp")
    up_full = gather_rows(gate_weight[1].astype(bf16), "dp")
    down_full = gather_rows(down_weight.T.astype(bf16), "dp")

    other_cotan = to_partner(cotangent)
    lo, hi, info = layout_of(seq_ids, block_ids, TILE, TILE)
    cosine, sine_table = rope_tables(lo)
    lo_col, hi_col = lo[:, None], hi[:, None]
    cotan_copies = copies_of(cotangent)
    cosine, sine_table, lo_col, hi_col, info, cotan_copies = lax.optimization_barrier(
        (cosine, sine_table, lo_col, hi_col, info, cotan_copies)
    )
    mark = tick(cosine, sine_table, lo_col, hi_col, info, cotan_copies)
    cotan_all = spread_rows(after(cotan_copies, normed_all))
    normed_all = after(normed_all, mark)
    order = jnp.argsort(groups, stable=True).astype(jnp.int32)

    projected = dot(normed_all, qkv_full)
    mixed_all, queries, keys_all, values_all, logsums = attn_fwd(
        info, projected, cosine, sine_table, lo_col, hi_col, TILE, TILE
    )
    attn_rows = sum_rows(dot_cols(mixed_all, out_full).astype(bf16))
    residual = field_in + attn_rows
    normed_two, scaled_two, factor_two = normed(residual, norm_gains[1])
    other_two = to_partner(normed_two)
    normed_two, gate_full, up_full = lax.optimization_barrier((normed_two, gate_full, up_full, tick(normed_two)))[:3]
    ffn_input = spread_rows(copies_of(normed_two))
    other_dy = gather_rows(after(other_cotan, ffn_input), "tensor")
    other_input = spread_rows(copies_of(after(other_two, ffn_input)))

    gate_pre = dot(ffn_input, gate_full)
    up_pre = dot(after(ffn_input, tick(gate_pre)), up_full)
    sigmoid_gate = jax.nn.sigmoid(gate_pre)
    swish = gate_pre * sigmoid_gate
    hidden = (swish * up_pre).astype(bf16)
    down_grad = dot_rows(half_cols(cotan_all), hidden).astype(bf16)
    down_recv = to_half(down_grad)
    hidden_grad = dot(after(cotan_all, down_grad), down_full)
    gate_grad_low = (
        hidden_grad * up_pre * sigmoid_gate * (1.0 + gate_pre * (1.0 - sigmoid_gate))
    ).astype(bf16)
    up_grad_low = (hidden_grad * swish).astype(bf16)
    ffn_back = (dot_cols(gate_grad_low, gate_full) + dot_cols(up_grad_low, up_full)).astype(bf16)
    ffn_back_rows = scatter_rows(ffn_back)
    mark = tick(ffn_back)
    input_half = half_cols(after(ffn_input, mark))
    gate_grad = dot_rows(input_half, gate_grad_low).astype(bf16)
    gate_recv = to_half(gate_grad)
    up_grad = dot_rows(input_half, up_grad_low).astype(bf16)
    up_recv = to_half(up_grad)
    hidden_own = hidden

    other_input = after(other_input, gate_grad, up_grad)
    gate_pre = dot(other_input, gate_full)
    up_pre = dot(after(other_input, tick(gate_pre)), up_full)
    sigmoid_gate = jax.nn.sigmoid(gate_pre)
    swish = gate_pre * sigmoid_gate
    hidden = (swish * up_pre).astype(bf16)
    mark = tick(hidden)
    other_dy = after(other_dy, mark)
    near = lax.axis_size("dp") // 2
    down_grad = dot_rows(half_cols(other_dy), hidden).astype(bf16)
    hidden_grad = dot(after(other_dy, down_grad), down_full)
    gate_grad_low = (
        hidden_grad * up_pre * sigmoid_gate * (1.0 + gate_pre * (1.0 - sigmoid_gate))
    ).astype(bf16)
    up_grad_low = (hidden_grad * swish).astype(bf16)
    input_half = half_cols(after(other_input, tick(gate_grad_low, up_grad_low)))
    rest = [dot_rows(input_half, low).astype(bf16) for low in (gate_grad_low, up_grad_low)]
    rest = jnp.stack([x.reshape(near, -1, x.shape[1]) for x in rest + [down_grad]], axis=1)
    rest_recv = to_half(rest.reshape(-1, rest.shape[-1]))
    mark = tick(rest)

    cotan_rows = cotangent.astype(jnp.float32)
    resid_grad = cotan_rows + norm_back(ffn_back_rows, scaled_two, factor_two, norm_gains[1])
    gain_two = jnp.sum(ffn_back_rows * scaled_two, axis=0)
    resid_all = gather_rows(resid_grad.astype(bf16), "tensor")
    resid_all = after(resid_all, mark)
    mixed_grad = dot(resid_all, out_full).astype(bf16)
    out_grad = dot_rows(resid_all, mixed_all).astype(bf16)
    out_recv = to_owners(out_grad)
    mixed_grad = after(mixed_grad, out_grad)
    raw_grads = attn_bwd(
        info, queries, keys_all, values_all, mixed_all, mixed_grad, logsums,
        cosine, sine_table, lo[None], hi[None], TILE, TILE,
    )
    raw_all = jnp.concatenate(raw_grads, axis=1)
    in_grad = dot_cols(raw_all, qkv_full).astype(bf16)
    in_grad_rows = scatter_rows(in_grad)
    qkv_grad = dot_rows(after(normed_all, tick(in_grad)), raw_all).astype(bf16)
    qkv_recv = to_owners(qkv_grad)
    ffn_part = scatter_rows(dot_cols(after(hidden_own, qkv_grad), down_full))
    layer_out = (residual + ffn_part).astype(bf16)
    tokens_grad = resid_grad + norm_back(in_grad_rows, scaled_one, factor_one, norm_gains[0])
    gain_one = jnp.sum(in_grad_rows * scaled_one, axis=0)
    gain_part = jnp.stack([gain_one, gain_two])
    gain_part = jnp.sum(lax.all_gather(gain_part, "tensor", axis=0), axis=0)
    gain_all = lax.all_gather(gain_part, "dp", axis=0)
    picker = groups[None, :] == jnp.arange(GROUPS, dtype=jnp.int32)[:, None]
    gain_grad = jnp.sum(jnp.where(picker[:, :, None, None], gain_all[None], 0.0), axis=1)
    order = after(order, gain_all)
    side = order // near != lax.axis_index("dp") // near
    near_order = order % near + near * side.astype(jnp.int32)

    down_new = optimize(
        near_order, (down_recv, rest_recv), down_weight, down_first, down_second, down_outer, 3, turned=True
    )
    gate_half = optimize(
        near_order, (gate_recv, rest_recv), gate_weight, gate_first, gate_second, gate_outer, 2, member=0
    )
    gate_new = optimize(
        near_order, (up_recv, rest_recv), gate_weight, gate_first, gate_second, gate_outer, 2, member=1, before=gate_half
    )
    out_new = optimize(
        order, (out_recv,), out_weight, out_first, out_second, out_outer, 1, turned=True
    )
    qkv_new = optimize(
        order, (qkv_recv,), qkv_weight, qkv_first, qkv_second, qkv_outer, 0
    )
    gains_new = update(
        norm_gains, gain_grad, gains_first, gains_second, gains_outer, inner_rates[4], decays[4]
    )
    return (layer_out, tokens_grad, *qkv_new, *out_new, *gate_new, *down_new, *gains_new)


def solution(mesh):
    in_specs = (
        P(("dp", "tensor"), None),
        P(("dp", "tensor"), None),
        P("dp"),
        P("dp"),
        P(),
        P(None, "dp", "tensor"),
        P("tensor", "dp"),
        P(None, "dp", "tensor"),
        P("tensor", "dp"),
        P(),
        P(None, None, "dp", "tensor"),
        P(None, "tensor", "dp"),
        P(None, None, "dp", "tensor"),
        P(None, "tensor", "dp"),
        P(),
        P(None, None, "dp", "tensor"),
        P(None, "tensor", "dp"),
        P(None, None, "dp", "tensor"),
        P(None, "tensor", "dp"),
        P(),
        P(None, "dp", "tensor"),
        P("tensor", "dp"),
        P(None, "dp", "tensor"),
        P("tensor", "dp"),
        P(),
    )
    out_specs = (
        P(("dp", "tensor"), None),
        P(("dp", "tensor"), None),
        P(None, None, "dp", "tensor"),
        P(None, None, "dp", "tensor"),
        P(None, "dp", "tensor"),
        P(None, "dp", "tensor"),
        P(None, "dp", "tensor"),
        P(None, "dp", "tensor"),
        P(None, "tensor", "dp"),
        P(None, "tensor", "dp"),
        P("tensor", "dp"),
        P("tensor", "dp"),
        P("tensor", "dp"),
        P("tensor", "dp"),
        P(None, None, "dp", "tensor"),
        P(None, None, "dp", "tensor"),
        P(None, "dp", "tensor"),
        P(None, "dp", "tensor"),
        P(None, "dp", "tensor"),
        P(None, "dp", "tensor"),
        P(None, "tensor", "dp"),
        P(None, "tensor", "dp"),
        P("tensor", "dp"),
        P("tensor", "dp"),
        P("tensor", "dp"),
        P("tensor", "dp"),
        P(),
        P(),
        P(),
        P(),
        P(),
        P(),
    )
    return jax.shard_map(step, mesh=mesh, in_specs=in_specs, out_specs=out_specs, check_vma=False)
```

```python
import functools

import jax
import jax.numpy as jnp
from jax import lax
from jax.experimental import pallas as pl
from jax.experimental.pallas import tpu as pltpu
from jax.sharding import PartitionSpec as P

NT = (((1,), (1,)), ((), ()))
TN = (((0,), (0,)), ((), ()))
NEG = -1e30
LANES = 128


def swap_halves(u):
    lane = lax.broadcasted_iota(jnp.int32, u.shape, 1)
    return jnp.where(lane % 64 < 32, pltpu.roll(u, 96, 1), pltpu.roll(u, 32, 1))


def head_parts(u):
    lane = lax.broadcasted_iota(jnp.int32, u.shape, 1)
    zero = jnp.zeros_like(u)
    return jnp.where(lane < 64, u, zero), jnp.where(lane < 64, zero, u)


def fwd_kernel(tq, tk, info, q_ref, k_ref, v_ref, cos_ref, sin_ref, lo_ref, hi_ref,
               o_ref, qr_ref, kr_ref, vr_ref, lse_ref, q2, v2, m_s, l_s, acc):
    rows = q_ref.shape[0]
    step = 256
    def prep(i, c):
        at = pl.ds(pl.multiple_of(i * step, step), step)
        cos, sin = cos_ref[at, :], sin_ref[at, :]
        q = q_ref[at, :]
        q = (q * cos + swap_halves(q) * sin).astype(jnp.bfloat16) * jnp.bfloat16(0.125)
        k = k_ref[at, :]
        k = (k * cos + swap_halves(k) * sin).astype(jnp.bfloat16)
        v = v_ref[at, :].astype(jnp.bfloat16)
        qr_ref[at, :] = q
        kr_ref[at, :] = k
        vr_ref[at, :] = v
        q2[0, at, :], q2[1, at, :] = head_parts(q)
        v2[0, at, :], v2[1, at, :] = head_parts(v)
        return c
    lax.fori_loop(0, rows // step, prep, 0)

    def q_tile(i, c):
        at = pl.ds(pl.multiple_of(i * tq, tq), tq)
        m_s[...] = jnp.full_like(m_s, -1e29)
        l_s[...] = jnp.zeros_like(l_s)
        acc[...] = jnp.zeros_like(acc)
        first = info[0, i] // tk
        last = (info[3, i] + tk - 1) // tk

        def tile(j, masked):
            ks = pl.multiple_of(j * tk, tk)
            kat = pl.ds(ks, tk)
            k = kr_ref[kat, :]
            if masked:
                key = lax.broadcasted_iota(jnp.int32, (tq, tk), 1) + ks
                ok = (key >= lo_ref[at, :]) & (key < hi_ref[at, :])
            for h in range(2):
                s = lax.dot_general(q2[h, at, :], k, NT, preferred_element_type=jnp.float32)
                if masked:
                    s = jnp.where(ok, s, NEG)
                m_old = m_s[h]
                m_new = jnp.maximum(m_old, jnp.max(s, axis=1, keepdims=True))
                p = jnp.exp(s - m_new[:, :1])
                alpha = jnp.exp(m_old - m_new)
                l_s[h] = alpha * l_s[h] + jnp.sum(p, axis=1, keepdims=True)
                acc[h] = acc[h] * alpha + jnp.dot(
                    p.astype(jnp.bfloat16), v2[h, kat, :], preferred_element_type=jnp.float32)
                m_s[h] = m_new

        def kv_tile(j, c):
            ks = j * tk
            full = (info[1, i] <= ks) & (info[2, i] >= ks + tk)
            @pl.when(full)
            def _():
                tile(j, False)
            @pl.when(jnp.logical_not(full))
            def _():
                tile(j, True)
            return c
        lax.fori_loop(first, last, kv_tile, 0)
        l0, l1 = l_s[0], l_s[1]
        o_ref[at, :] = (acc[0] / l0 + acc[1] / l1).astype(jnp.bfloat16)
        lane = lax.broadcasted_iota(jnp.int32, (tq, LANES), 1)
        lse = jnp.where(lane < 64, m_s[0] + jnp.log(l0), m_s[1] + jnp.log(l1))
        flat = lse.T
        lse_ref[0, 0:1, at] = flat[0:1, :]
        lse_ref[0, 1:2, at] = flat[64:65, :]
        return c
    lax.fori_loop(0, rows // tq, q_tile, 0)


def attn_fwd(info, proj, cos, sin, lo, hi, tq, tk):
    rows, width = proj.shape
    pairs = width // 3 // LANES
    full = lambda p: (0, 0)
    blk = (rows, LANES)
    outs = [jax.ShapeDtypeStruct((rows, pairs * LANES), jnp.bfloat16)] * 4 + [
        jax.ShapeDtypeStruct((pairs, 2, rows), jnp.float32)]
    pair_spec = pl.BlockSpec(blk, lambda p: (0, p))
    area = rows * rows * pairs * 2 * 0.6
    return pl.pallas_call(
        functools.partial(fwd_kernel, tq, tk),
        out_shape=outs,
        grid=(pairs,),
        in_specs=[
            pl.BlockSpec(memory_space=pltpu.SMEM),
            pl.BlockSpec(blk, lambda p: (0, p)),
            pl.BlockSpec(blk, lambda p: (0, p + pairs)),
            pl.BlockSpec(blk, lambda p: (0, p + 2 * pairs)),
            pl.BlockSpec(blk, full), pl.BlockSpec(blk, full),
            pl.BlockSpec((rows, 1), full), pl.BlockSpec((rows, 1), full)],
        out_specs=[pair_spec] * 4 + [pl.BlockSpec((1, 2, rows), lambda p: (p, 0, 0))],
        scratch_shapes=[pltpu.VMEM((2, rows, LANES), jnp.bfloat16), pltpu.VMEM((2, rows, LANES), jnp.bfloat16),
                        pltpu.VMEM((2, tq, LANES), jnp.float32), pltpu.VMEM((2, tq, LANES), jnp.float32),
                        pltpu.VMEM((2, tq, LANES), jnp.float32)],
        compiler_params=pltpu.CompilerParams(vmem_limit_bytes=48 << 20),
        cost_estimate=pl.CostEstimate(flops=int(4 * area * 64), transcendentals=int(area), bytes_accessed=rows * width * 4),
        name="attn_fwd",
    )(info, proj, proj, proj, cos, sin, lo, hi)


def bwd_kernel(tq, tk, info, q_ref, k_ref, v_ref, o_ref, do_ref, lse_ref, cos_ref, sin_ref, lo_ref, hi_ref,
               dq_ref, dk_ref, dv_ref, q2, k2, v2, g2, delta, dq_acc, dk_acc, dv_acc):
    rows = q_ref.shape[0]
    step = 256
    def prep(i, c):
        at = pl.ds(pl.multiple_of(i * step, step), step)
        q2[0, at, :], q2[1, at, :] = head_parts(q_ref[at, :])
        k2[0, at, :], k2[1, at, :] = head_parts(k_ref[at, :])
        v2[0, at, :], v2[1, at, :] = head_parts(v_ref[at, :])
        g = do_ref[at, :]
        g2[0, at, :], g2[1, at, :] = head_parts(g)
        prod = (g.astype(jnp.float32) * o_ref[at, :].astype(jnp.float32)).T
        delta[0:1, at] = jnp.sum(prod[:64], axis=0, keepdims=True)
        delta[1:2, at] = jnp.sum(prod[64:], axis=0, keepdims=True)
        dq_acc[at, :] = jnp.zeros((step, LANES), jnp.float32)
        return c
    lax.fori_loop(0, rows // step, prep, 0)

    def k_tile(j, c):
        ks = pl.multiple_of(j * tk, tk)
        kat = pl.ds(ks, tk)
        dk_acc[...] = jnp.zeros_like(dk_acc)
        dv_acc[...] = jnp.zeros_like(dv_acc)
        first = info[4, j] // tq
        last = (info[5, j] + tq - 1) // tq

        def tile(i, masked):
            at = pl.ds(pl.multiple_of(i * tq, tq), tq)
            if masked:
                key = lax.broadcasted_iota(jnp.int32, (tk, tq), 0) + ks
                ok = (key >= lo_ref[0:1, at]) & (key < hi_ref[0:1, at])
            for h in range(2):
                kh, qh, gh = k2[h, kat, :], q2[h, at, :], g2[h, at, :]
                s = lax.dot_general(kh, qh, NT, preferred_element_type=jnp.float32)
                if masked:
                    s = jnp.where(ok, s, NEG)
                p = jnp.exp(s - lse_ref[0, h:h + 1, at])
                dp = lax.dot_general(v2[h, kat, :], gh, NT, preferred_element_type=jnp.float32)
                ds = (p * (dp - delta[h:h + 1, at])).astype(jnp.bfloat16)
                dv_acc[...] += jnp.dot(p.astype(jnp.bfloat16), gh, preferred_element_type=jnp.float32)
                dk_acc[...] += jnp.dot(ds, qh, preferred_element_type=jnp.float32)
                dq_acc[at, :] += lax.dot_general(ds, kh, TN, preferred_element_type=jnp.float32)

        def q_loop(i, c):
            full = (info[1, i] <= ks) & (info[2, i] >= ks + tk)
            @pl.when(full)
            def _():
                tile(i, False)
            @pl.when(jnp.logical_not(full))
            def _():
                tile(i, True)
            return c
        lax.fori_loop(first, last, q_loop, 0)
        cos, sin = cos_ref[kat, :], sin_ref[kat, :]
        dk = dk_acc[...]
        dk_ref[kat, :] = (dk * cos - swap_halves(dk) * sin).astype(jnp.bfloat16)
        dv_ref[kat, :] = dv_acc[...].astype(jnp.bfloat16)
        return c
    lax.fori_loop(0, rows // tk, k_tile, 0)

    def finish(i, c):
        at = pl.ds(pl.multiple_of(i * step, step), step)
        dq = dq_acc[at, :] * 0.125
        dq_ref[at, :] = (dq * cos_ref[at, :] - swap_halves(dq) * sin_ref[at, :]).astype(jnp.bfloat16)
        return c
    lax.fori_loop(0, rows // step, finish, 0)


def attn_bwd(info, q, k, v, o, do, lse, cos, sin, lo, hi, tq, tk):
    rows, width = q.shape
    pairs = width // LANES
    full = lambda p: (0, 0)
    blk = (rows, LANES)
    pair_spec = pl.BlockSpec(blk, lambda p: (0, p))
    area = rows * rows * pairs * 2 * 0.6
    return pl.pallas_call(
        functools.partial(bwd_kernel, tq, tk),
        out_shape=[jax.ShapeDtypeStruct((rows, width), jnp.bfloat16)] * 3,
        grid=(pairs,),
        in_specs=[pl.BlockSpec(memory_space=pltpu.SMEM)] + [pair_spec] * 5 + [
            pl.BlockSpec((1, 2, rows), lambda p: (p, 0, 0)),
            pl.BlockSpec(blk, full), pl.BlockSpec(blk, full),
            pl.BlockSpec((1, rows), full), pl.BlockSpec((1, rows), full)],
        out_specs=[pair_spec] * 3,
        scratch_shapes=[pltpu.VMEM((2, rows, LANES), jnp.bfloat16)] * 4 + [
            pltpu.VMEM((2, rows), jnp.float32), pltpu.VMEM((rows, LANES), jnp.float32),
            pltpu.VMEM((tk, LANES), jnp.float32), pltpu.VMEM((tk, LANES), jnp.float32)],
        compiler_params=pltpu.CompilerParams(vmem_limit_bytes=48 << 20),
        cost_estimate=pl.CostEstimate(flops=int(10 * area * 64), transcendentals=int(area), bytes_accessed=rows * width * 16),
        name="attn_bwd",
    )(info, q, k, v, o, do, lse, cos, sin, lo, hi)


def layout_of(seq, block, tq, tk):
    rows = seq.shape[0]
    code = seq * 8 + block
    lo = jnp.sum((seq[None, :] < seq[:, None]).astype(jnp.int32), axis=1)
    hi = jnp.sum((code[None, :] <= code[:, None]).astype(jnp.int32), axis=1)
    lt, ht = lo.reshape(-1, tq), hi.reshape(-1, tq)
    start = jnp.arange(rows // tk, dtype=jnp.int32)[:, None] * tk
    qlo = jnp.sum((hi[None, :] <= start).astype(jnp.int32), axis=1)
    qhi = jnp.sum((lo[None, :] < start + tk).astype(jnp.int32), axis=1)
    info = jnp.stack([lt.min(1), lt.max(1), ht.min(1), ht.max(1), qlo, qhi]) if tq == tk else None
    return lo, hi, info


def rope_tables(lo, base=130000.0):
    rows = lo.shape[0]
    where_at = (jnp.arange(rows, dtype=jnp.int32) - lo).astype(jnp.float32)
    inverse = base ** (-(jnp.arange(32, dtype=jnp.float32) * 2.0 / 64))
    ang = where_at[:, None] * inverse[None, :]
    cos, sin = jnp.cos(ang), jnp.sin(ang)
    return jnp.concatenate([cos] * 4, axis=1), jnp.concatenate([-sin, sin, -sin, sin], axis=1)


DP, TP = "dp", "tensor"
GROUPS = 4
STEP = 4

norm_eps = 1e-05
beta_first = 0.9
beta_second = 0.95
adam_eps = 1e-08
outer_rate = 0.7
outer_beta = 0.9
inner_rates = (0.04, 0.6, 0.04, 0.02, 0.35)
decays = (0.1, 0.1, 0.1, 0.1, 0.0)
fix_first = 1.0 - beta_first**STEP
fix_second = 1.0 - beta_second**STEP
TILE = 512


def normed(field_rows, gain_row):
    factor = lax.rsqrt(jnp.mean(field_rows * field_rows, axis=-1, keepdims=True) + norm_eps)
    scaled = field_rows * factor
    return ((scaled * gain_row).astype(jnp.bfloat16), scaled, factor)


def norm_back(upstream, scaled, factor, gain_row):
    inside = upstream * gain_row
    return factor * (inside - scaled * jnp.mean(inside * scaled, axis=-1, keepdims=True))


def update(weight, gradient, first_old, second_old, outer_old, step_rate, decay_rate):
    first_new = beta_first * first_old + (1.0 - beta_first) * gradient
    second_new = beta_second * second_old + (1.0 - beta_second) * gradient * gradient
    ratio = first_new / fix_first / (jnp.sqrt(second_new / fix_second) + adam_eps)
    change = step_rate * (jnp.mean(ratio, axis=0) + decay_rate * weight)
    outer_new = outer_beta * outer_old + change
    master = weight - outer_rate * (change + outer_beta * outer_new)
    return [first_new, second_new, change, outer_new, master, master.astype(jnp.bfloat16)]


def opt_kernel(per, turned, parts, rate, decay, order, *refs):
    recvs, (first, second, weight, outer) = refs[:parts], refs[parts : parts + 4]
    first_new, second_new, delta, outer_new, master, low = refs[-6:]
    held = recvs[0].shape[0]
    rows, cols = weight.shape[-2:]
    step_r, step_c = min(rows, 16), min(cols, 256)
    if turned:
        step_r, step_c = min(rows, 128), min(cols, 128)
    lead = (0,) * (len(weight.shape) - 2)

    def chunk(i, carry):
        r = pl.multiple_of((i // (cols // step_c)) * step_r, step_r)
        c = pl.multiple_of((i % (cols // step_c)) * step_c, step_c)
        at = (pl.ds(r, step_r), pl.ds(c, step_c))
        w = weight[lead + at]
        total = jnp.zeros_like(w)
        for g in range(GROUPS):
            grad = None
            for j in range(per):
                source = order[g * per + j]
                block = (pl.ds(c, step_c), pl.ds(r, step_r)) if turned else at
                if parts == 1:
                    part = recvs[0][(source,) + block].astype(jnp.float32)
                else:
                    slot = lax.rem(source, held)
                    own, other = (x[(slot,) + block].astype(jnp.float32) for x in recvs)
                    part = jnp.where(source < held, own, other)
                grad = part if grad is None else grad + part
            if turned:
                grad = grad.T
            m = beta_first * first[(g,) + lead + at] + (1.0 - beta_first) * grad
            v = beta_second * second[(g,) + lead + at] + (1.0 - beta_second) * grad * grad
            first_new[(g,) + lead + at] = m
            second_new[(g,) + lead + at] = v
            total = total + m / (jnp.sqrt(v * (1.0 / fix_second)) + adam_eps)
        change = rate * (total * (1.0 / (fix_first * GROUPS)) + decay * w)
        moved = outer_beta * outer[lead + at] + change
        fresh = w - outer_rate * (change + outer_beta * moved)
        delta[lead + at] = change
        outer_new[lead + at] = moved
        master[lead + at] = fresh
        low[lead + at] = fresh.astype(jnp.bfloat16)
        return carry

    lax.fori_loop(0, (rows // step_r) * (cols // step_c), chunk, 0)


def optimize(order, recv, weight, first, second, outer, position, turned=False, member=None, before=None):
    held = recv[0].shape[0]
    sources = held * len(recv)
    stacked = weight.ndim == 3
    rows, cols = weight.shape[-2:]
    members = weight.shape[0] if stacked and member is None else 1
    base = member or 0
    area = 65536
    if turned:
        br, bc = max(128, min(rows, area // cols)), cols
    else:
        br, bc = max(16, min(rows, area // cols)), cols
    blocks = rows // br
    lead = (1,) if stacked else ()

    def pick(m):
        return (base + m,) if stacked else ()

    if turned:
        recv_spec = pl.BlockSpec((held, bc, br), lambda m, i: (0, 0, i))
    else:
        recv_spec = pl.BlockSpec((held, br, bc), lambda m, i: (0, i, m))
    recv_specs = [recv_spec]
    if len(recv) > 1:
        if turned:
            recv_specs.append(recv_spec)
        else:
            recv_specs.append(pl.BlockSpec((held, br, bc), lambda m, i: (0, base * blocks + i, 0)))
    one = pl.BlockSpec(lead + (br, bc), lambda m, i: pick(m) + (i, 0))
    many = pl.BlockSpec((GROUPS,) + lead + (br, bc), lambda m, i: (0,) + pick(m) + (i, 0))
    f32 = jnp.float32
    outs = [
        jax.ShapeDtypeStruct(first.shape, f32),
        jax.ShapeDtypeStruct(first.shape, f32),
        jax.ShapeDtypeStruct(weight.shape, f32),
        jax.ShapeDtypeStruct(weight.shape, f32),
        jax.ShapeDtypeStruct(weight.shape, f32),
        jax.ShapeDtypeStruct(weight.shape, jnp.bfloat16),
    ]
    operands = [order, *recv, first, second, weight, outer]
    specs = [pl.BlockSpec(memory_space=pltpu.SMEM)] + recv_specs + [many, many, one, one]
    aliases = {}
    if before is not None:
        aliases = {len(operands) + k: k for k in range(6)}
        operands += list(before)
        specs += [pl.BlockSpec(memory_space=pl.ANY)] * 6
    count = members * rows * cols
    return pl.pallas_call(
        functools.partial(
            opt_kernel, sources // GROUPS, turned, len(recv), inner_rates[position], decays[position]
        ),
        out_shape=outs,
        grid=(members, blocks),
        in_specs=specs,
        out_specs=[many, many, one, one, one, one],
        input_output_aliases=aliases,
        compiler_params=pltpu.CompilerParams(vmem_limit_bytes=40 << 20),
        cost_estimate=pl.CostEstimate(
            flops=60 * count, transcendentals=8 * count, bytes_accessed=(86 + 2 * sources) * count
        ),
        name="optimize",
    )(*operands)


def dot(left, right):
    return jnp.dot(left, right, preferred_element_type=jnp.float32)


def dot_cols(left, right):
    return lax.dot_general(left, right, (((1,), (1,)), ((), ())), preferred_element_type=jnp.float32)


def dot_rows(left, right):
    return lax.dot_general(left, right, (((0,), (0,)), ((), ())), preferred_element_type=jnp.float32)


def after(value, *others):
    return lax.optimization_barrier((value,) + others)[0]


def tick_kernel(*refs):
    refs[-1][...] = jnp.zeros_like(refs[-1])


def tick(*values):
    return pl.pallas_call(
        tick_kernel,
        out_shape=jax.ShapeDtypeStruct((8, LANES), jnp.float32),
        in_specs=[pl.BlockSpec(memory_space=pl.ANY)] * len(values),
        compiler_params=pltpu.CompilerParams(has_side_effects=True),
    )(*values)


def gather_rows(part, axis):
    return lax.all_gather(part, axis, axis=0, tiled=True)


def copies_of(part):
    return jnp.broadcast_to(part[None], (lax.axis_size(TP),) + part.shape)


def spread_rows(copies):
    parts = lax.all_to_all(copies, TP, split_axis=0, concat_axis=0)
    return parts.reshape((-1,) + copies.shape[2:])


def sum_rows(part):
    count = lax.axis_size(TP)
    blocks = part.reshape((count, part.shape[0] // count) + part.shape[1:])
    parts = lax.all_to_all(blocks, TP, split_axis=0, concat_axis=0)
    return jnp.sum(parts.astype(jnp.float32), axis=0)


def scatter_rows(part):
    summed = lax.psum_scatter(
        part.astype(jnp.bfloat16), TP, scatter_dimension=0, tiled=True
    )
    return summed.astype(jnp.float32)


def to_half(grad):
    count = lax.axis_size(DP)
    near = count // 2
    blocks = grad.astype(jnp.bfloat16).reshape((near, grad.shape[0] // near) + grad.shape[1:])
    halves = [list(range(near)), list(range(near, count))]
    return lax.all_to_all(blocks, DP, split_axis=0, concat_axis=0, axis_index_groups=halves)


def to_partner(part):
    count = lax.axis_size(DP)
    return lax.ppermute(part, DP, [(i, (i + count // 2) % count) for i in range(count)])


def half_cols(rows):
    near = lax.axis_size(DP) // 2
    wide = rows.shape[1] // 2
    return lax.dynamic_slice_in_dim(rows, lax.axis_index(DP) // near * wide, wide, axis=1)


def to_owners(grad):
    count = lax.axis_size(DP)
    blocks = grad.astype(jnp.bfloat16).reshape((count, grad.shape[0] // count) + grad.shape[1:])
    return lax.all_to_all(blocks, DP, split_axis=0, concat_axis=0)


def step(
    tokens,
    cotangent,
    seq_ids,
    block_ids,
    groups,
    qkv_weight,
    out_weight,
    gate_weight,
    down_weight,
    norm_gains,
    qkv_first,
    out_first,
    gate_first,
    down_first,
    gains_first,
    qkv_second,
    out_second,
    gate_second,
    down_second,
    gains_second,
    qkv_outer,
    out_outer,
    gate_outer,
    down_outer,
    gains_outer,
):
    bf16 = jnp.bfloat16
    field_in = tokens.astype(jnp.float32)
    normed_one, scaled_one, factor_one = normed(field_in, norm_gains[0])
    normed_all = spread_rows(copies_of(normed_one))
    qkv_full = gather_rows(jnp.concatenate([qkv_weight[m].astype(bf16) for m in range(3)], axis=1), DP)
    out_full = gather_rows(out_weight.T.astype(bf16), DP)
    gate_full = gather_rows(gate_weight[0].astype(bf16), DP)
    up_full = gather_rows(gate_weight[1].astype(bf16), DP)
    down_full = gather_rows(down_weight.T.astype(bf16), DP)

    other_cotan = to_partner(cotangent)
    lo, hi, info = layout_of(seq_ids, block_ids, TILE, TILE)
    cosine, sine_table = rope_tables(lo)
    lo_col, hi_col = lo[:, None], hi[:, None]
    cotan_copies = copies_of(cotangent)
    cosine, sine_table, lo_col, hi_col, info, cotan_copies = lax.optimization_barrier(
        (cosine, sine_table, lo_col, hi_col, info, cotan_copies)
    )
    mark = tick(cosine, sine_table, lo_col, hi_col, info, cotan_copies)
    cotan_all = spread_rows(after(cotan_copies, normed_all))
    normed_all = after(normed_all, mark)
    order = jnp.argsort(groups, stable=True).astype(jnp.int32)

    projected = dot(normed_all, qkv_full)
    mixed_all, queries, keys_all, values_all, logsums = attn_fwd(
        info, projected, cosine, sine_table, lo_col, hi_col, TILE, TILE
    )
    attn_rows = sum_rows(dot_cols(mixed_all, out_full).astype(bf16))
    residual = field_in + attn_rows
    normed_two, scaled_two, factor_two = normed(residual, norm_gains[1])
    normed_two, gate_full, up_full = lax.optimization_barrier((normed_two, gate_full, up_full))
    ffn_input = spread_rows(copies_of(normed_two))
    other_two = to_partner(after(normed_two, down_full))
    mark = tick(ffn_input)
    ffn_input = after(ffn_input, mark)
    other_dy = gather_rows(other_cotan, TP)
    other_input = gather_rows(other_two, TP)

    gate_pre = dot(ffn_input, gate_full)
    up_pre = dot(ffn_input, up_full)
    sigmoid_gate = jax.nn.sigmoid(gate_pre)
    swish = gate_pre * sigmoid_gate
    hidden = (swish * up_pre).astype(bf16)
    down_grad = dot_rows(half_cols(cotan_all), hidden).astype(bf16)
    down_recv = to_half(down_grad)
    hidden_grad = dot(after(cotan_all, tick(down_grad)), down_full)
    gate_grad_low = (
        hidden_grad * up_pre * sigmoid_gate * (1.0 + gate_pre * (1.0 - sigmoid_gate))
    ).astype(bf16)
    up_grad_low = (hidden_grad * swish).astype(bf16)
    ffn_back = (dot_cols(gate_grad_low, gate_full) + dot_cols(up_grad_low, up_full)).astype(bf16)
    ffn_back_rows = scatter_rows(ffn_back)
    input_half = half_cols(after(ffn_input, ffn_back))
    gate_grad = dot_rows(input_half, gate_grad_low).astype(bf16)
    gate_recv = to_half(gate_grad)
    up_grad = dot_rows(input_half, up_grad_low).astype(bf16)
    up_recv = to_half(up_grad)
    hidden_own = hidden

    other_input = after(other_input, gate_grad, up_grad)
    gate_pre = dot(other_input, gate_full)
    up_pre = dot(other_input, up_full)
    sigmoid_gate = jax.nn.sigmoid(gate_pre)
    swish = gate_pre * sigmoid_gate
    hidden = (swish * up_pre).astype(bf16)
    mark = tick(hidden)
    other_dy = after(other_dy, mark)
    near = lax.axis_size(DP) // 2
    down_grad = dot_rows(half_cols(other_dy), hidden).astype(bf16)
    down_recv2 = to_half(down_grad)
    hidden_grad = dot(after(other_dy, down_grad), down_full)
    gate_grad_low = (
        hidden_grad * up_pre * sigmoid_gate * (1.0 + gate_pre * (1.0 - sigmoid_gate))
    ).astype(bf16)
    up_grad_low = (hidden_grad * swish).astype(bf16)
    input_half = half_cols(after(other_input, tick(gate_grad_low, up_grad_low)))
    rest = [dot_rows(input_half, low).astype(bf16) for low in (gate_grad_low, up_grad_low)]
    rest = jnp.stack([x.reshape(near, -1, x.shape[1]) for x in rest], axis=1)
    rest_recv = to_half(rest.reshape(-1, rest.shape[-1]))
    mark = tick(rest)

    cotan_rows = cotangent.astype(jnp.float32)
    resid_grad = cotan_rows + norm_back(ffn_back_rows, scaled_two, factor_two, norm_gains[1])
    gain_two = jnp.sum(ffn_back_rows * scaled_two, axis=0)
    resid_all = gather_rows(resid_grad.astype(bf16), TP)
    resid_all = after(resid_all, mark)
    mixed_grad = dot(resid_all, out_full).astype(bf16)
    out_grad = dot_rows(resid_all, mixed_all).astype(bf16)
    out_recv = to_owners(out_grad)
    mixed_grad = after(mixed_grad, out_grad)
    raw_grads = attn_bwd(
        info, queries, keys_all, values_all, mixed_all, mixed_grad, logsums,
        cosine, sine_table, lo[None], hi[None], TILE, TILE,
    )
    raw_all = jnp.concatenate(raw_grads, axis=1)
    in_grad = dot_cols(raw_all, qkv_full).astype(bf16)
    in_grad_rows = scatter_rows(in_grad)
    qkv_grad = dot_rows(after(normed_all, tick(in_grad)), raw_all).astype(bf16)
    qkv_recv = to_owners(qkv_grad)
    ffn_part = scatter_rows(dot_cols(after(hidden_own, qkv_grad), down_full))
    layer_out = (residual + ffn_part).astype(bf16)
    tokens_grad = resid_grad + norm_back(in_grad_rows, scaled_one, factor_one, norm_gains[0])
    gain_one = jnp.sum(in_grad_rows * scaled_one, axis=0)
    own_group = (jnp.arange(GROUPS, dtype=jnp.int32) == groups[lax.axis_index(DP)]).astype(
        jnp.float32
    )
    gain_slots = own_group[:, None, None] * jnp.stack([gain_one, gain_two])[None]
    gain_grad = lax.psum(gain_slots, (DP, TP))
    order = after(order, gain_slots)
    side = order // near != lax.axis_index(DP) // near
    near_order = order % near + near * side.astype(jnp.int32)

    down_new = optimize(
        near_order, (down_recv, down_recv2), down_weight, down_first, down_second, down_outer, 3, turned=True
    )
    gate_half = optimize(
        near_order, (gate_recv, rest_recv), gate_weight, gate_first, gate_second, gate_outer, 2, member=0
    )
    gate_new = optimize(
        near_order, (up_recv, rest_recv), gate_weight, gate_first, gate_second, gate_outer, 2, member=1, before=gate_half
    )
    out_new = optimize(
        order, (out_recv,), out_weight, out_first, out_second, out_outer, 1, turned=True
    )
    qkv_new = optimize(
        order, (qkv_recv,), qkv_weight, qkv_first, qkv_second, qkv_outer, 0
    )
    gains_new = update(
        norm_gains, gain_grad, gains_first, gains_second, gains_outer, inner_rates[4], decays[4]
    )
    return (layer_out, tokens_grad, *qkv_new, *out_new, *gate_new, *down_new, *gains_new)


def solution(mesh):
    in_specs = (
        P((DP, TP), None),
        P((DP, TP), None),
        P(DP),
        P(DP),
        P(),
        P(None, DP, TP),
        P(TP, DP),
        P(None, DP, TP),
        P(TP, DP),
        P(),
        P(None, None, DP, TP),
        P(None, TP, DP),
        P(None, None, DP, TP),
        P(None, TP, DP),
        P(),
        P(None, None, DP, TP),
        P(None, TP, DP),
        P(None, None, DP, TP),
        P(None, TP, DP),
        P(),
        P(None, DP, TP),
        P(TP, DP),
        P(None, DP, TP),
        P(TP, DP),
        P(),
    )
    out_specs = (
        P((DP, TP), None),
        P((DP, TP), None),
        P(None, None, DP, TP),
        P(None, None, DP, TP),
        P(None, DP, TP),
        P(None, DP, TP),
        P(None, DP, TP),
        P(None, DP, TP),
        P(None, TP, DP),
        P(None, TP, DP),
        P(TP, DP),
        P(TP, DP),
        P(TP, DP),
        P(TP, DP),
        P(None, None, DP, TP),
        P(None, None, DP, TP),
        P(None, DP, TP),
        P(None, DP, TP),
        P(None, DP, TP),
        P(None, DP, TP),
        P(None, TP, DP),
        P(None, TP, DP),
        P(TP, DP),
        P(TP, DP),
        P(TP, DP),
        P(TP, DP),
        P(),
        P(),
        P(),
        P(),
        P(),
        P(),
    )
    return jax.shard_map(step, mesh=mesh, in_specs=in_specs, out_specs=out_specs, check_vma=False)
```
